256 devices in a mesh: dom: 8 (over y, core), run: 32 (over x, z).
Axes of the slice: x: 4, y: 4, z: 8, core: 2. Of those that a mesh axis runs over, the one named last changes fastest.
Arguments:
- ainv: bfloat16 [1, 512, 2, 256, 256], P(None, ('dom', 'run')), as said below
- coupling: bfloat16 [512, 2, 256, 256], P(('dom', 'run')), as said below
- source: bfloat16 [1, 512, 2, 256, 128], P(None, ('dom', 'run')), may hold values from -0.5 to 0.5
Outputs:
- state: float32 [1, 512, 2, 256, 128], P(None, ('dom', 'run'))
The draws below stay inside these ranges and needn't reach their ends.
Inputs may be any that keep to these rules, and one draw needn't show every extreme that they name: Every block of ainv and of coupling is upper triangular in the orbital order; the diagonal entries of coupling are 1. Every block of coupling is upper triangular with unit diagonal.
All inputs are finite; a program needn't handle non-finite values.
Results may differ from the reference program's by a relative error of at most 0.0032.
Values sent between devices are 32-bit elements; how exact they have to be, the bound alone decides.
A program may use at most 128 MiB of HBM per device.

```python
import math
import jax
import jax.numpy as jnp
from jax import lax

ORB = 256
MODES = 128
ENERGIES = 1
SLABS = 512


def draw_ainv(key, part):
    keys = jax.random.split(key, 7)
    lowest = math.log(0.05 / SLABS)
    highest = math.log(0.3)
    spread = jax.random.uniform(keys[0], (ENERGIES, 1, ORB), jnp.float32)
    log_rate = lowest + (highest - lowest) * spread
    random_perturbation = jax.random.uniform(keys[1], (ENERGIES, SLABS, ORB), jnp.float32, 0.7, 1.4)
    decay_speed = jnp.exp(log_rate) * random_perturbation
    places = jax.random.randint(keys[2], (ENERGIES, 3), 0, SLABS)
    slab_ids = jnp.arange(SLABS)
    excited_sites = jnp.any(slab_ids[None, :, None] == places[:, None, :], axis=-1)
    damping_multiplier = jax.random.uniform(keys[3], (ENERGIES, SLABS), jnp.float32, 0.5, 0.8)
    pulse_amplitude = jnp.where(excited_sites, damping_multiplier, 1.0)
    retained_fraction = jnp.exp(-decay_speed) * pulse_amplitude[:, :, None]
    phase = jax.random.uniform(keys[4], (ENERGIES, 1, ORB), jnp.float32, -math.pi, math.pi)
    phase = phase + 0.3 * jax.random.normal(keys[5], (ENERGIES, SLABS, ORB), jnp.float32)
    diag_pair = jnp.stack([retained_fraction * jnp.cos(phase), retained_fraction * jnp.sin(phase)], axis=2)
    rows = jnp.arange(ORB)
    upper = (rows[:, None] < rows[None, :]).astype(jnp.float32)
    column_scale = jnp.sqrt(jnp.maximum(1.0 - retained_fraction * retained_fraction, 0.0))
    noise = jax.random.normal(keys[6], (ENERGIES, SLABS, 2, ORB, ORB), jnp.float32)
    off_part = noise * (0.5 / math.sqrt(ORB)) * column_scale[:, :, None, None, :] * upper
    eye = jnp.eye(ORB, dtype=jnp.float32)
    whole = off_part + diag_pair[:, :, :, None, :] * eye
    return whole.astype(jnp.bfloat16)


def draw_coupling(key, part):
    keys = jax.random.split(key, 1)
    rows = jnp.arange(ORB)
    upper = (rows[:, None] < rows[None, :]).astype(jnp.float32)
    noise = jax.random.normal(keys[0], (SLABS, 2, ORB, ORB), jnp.float32) * (0.1 / math.sqrt(ORB)) * upper
    eye = jnp.eye(ORB, dtype=jnp.float32)
    unit = jnp.stack([eye, jnp.zeros_like(eye)], axis=0)
    return (noise + unit).astype(jnp.bfloat16)


def steps_of(key, shape, shards, least, high):
    def one(axis_at, parts):
        heights = jax.random.uniform(jax.random.fold_in(jax.random.fold_in(key, 6), axis_at), (parts,), jnp.float32, least / len(shards), high / len(shards))
        return jnp.repeat(jnp.exp(heights), shape[axis_at] // parts).reshape((-1,) + (1,) * (len(shape) - axis_at - 1))

    level = one(*shards[0])
    for cut in shards[1:]:
        level = level * one(*cut)
    return level


def bell_draw(rng, dims, scale, most, cuts=(), kind=jnp.bfloat16):
    loudness = steps_of(rng, dims, cuts, -0.22, 0.18) if cuts else 1.0
    result = jax.random.normal(rng, dims, jnp.float32) * scale * loudness
    return jnp.minimum(jnp.maximum(result, -most), most).astype(kind)


def setup_inputs(seed: int = 0) -> dict:
    key_list = jax.random.split(jax.random.key(seed), 4)
    return {
        "ainv": draw_ainv(jax.random.fold_in(key_list[3], 71), 0),
        "coupling": draw_coupling(jax.random.fold_in(key_list[3], 71), 0),
        "source": bell_draw(key_list[2], (ENERGIES, SLABS, 2, ORB, MODES), 0.08, 0.5, ((1, 256),)),
    }


def cprod(left, right):
    hp = lax.Precision.HIGHEST
    real = jnp.einsum('...ij,...jk->...ik', left[..., 0, :, :], right[..., 0, :, :], precision=hp) - jnp.einsum('...ij,...jk->...ik', left[..., 1, :, :], right[..., 1, :, :], precision=hp)
    imag = jnp.einsum('...ij,...jk->...ik', left[..., 0, :, :], right[..., 1, :, :], precision=hp) + jnp.einsum('...ij,...jk->...ik', left[..., 1, :, :], right[..., 0, :, :], precision=hp)
    return jnp.stack([real, imag], axis=-3)


def reference(ainv, coupling, source):
    def slab_step(carry, inputs):
        block, link, src = inputs
        inverse = block.astype(jnp.float32)
        hop = -cprod(inverse, link.astype(jnp.float32)[None])
        hop = lax.optimization_barrier(hop.astype(jnp.bfloat16)).astype(jnp.float32)
        injection_source = cprod(inverse, src.astype(jnp.float32))
        carry = cprod(hop, carry) + injection_source
        return carry, carry

    start = jnp.zeros((source.shape[0], 2, source.shape[3], source.shape[4]), jnp.float32)
    _, slab_state_list = lax.scan(slab_step, start, (jnp.moveaxis(ainv, 1, 0), coupling, jnp.moveaxis(source, 1, 0)))
    return jnp.moveaxis(slab_state_list, 0, 1)
```

```python
import jax
import jax.numpy as jnp
from jax import lax
from jax.experimental import pallas as pl
from jax.experimental.pallas import tpu as pltpu
from jax.sharding import PartitionSpec as P

MESH = pl.DeviceIdType.MESH
F32 = jnp.float32
BF16 = jnp.bfloat16

NX = 4
H = 128
R = 32
NA2 = H // R
NA11 = H // 2 // R
NB = H // R
A11_ROW = H
B_ROW = H + H // 2
ROWS = B_ROW + H
A11_CH = NA2
B_CH = NA2 + NA11
NC = B_CH + NB


def dot(a, b):
    return lax.dot_general(a, b, (((1,), (0,)), ((), ())), preferred_element_type=F32)


def split(x):
    hi = x.astype(BF16)
    return hi, (x - hi.astype(F32)).astype(BF16)


def rows(start, size):
    return pl.ds(pl.multiple_of(start, 8), size)


def put_tile(w, t, top):
    w[t, 0:H, :] = top
    w[t, H : 2 * H, 0:H] = -top[:, H:]
    w[t, H : 2 * H, H:] = top[:, :H]


def put_weights(w, buf):
    def one(t, top):
        hi, lo = split(top)
        put_tile(w.at[0], t, hi)
        put_tile(w.at[1], t, lo)

    a11 = buf[A11_ROW : A11_ROW + H // 2, :]
    one(0, jnp.concatenate([a11[:, : 2 * H], a11[:, 2 * H :]], axis=0))
    one(1, buf[0:H, 0 : 2 * H])
    one(2, buf[0:H, 2 * H :])


def mul3(x, w, t):
    n = x.shape[0]
    hi, lo = split(x)
    both = dot(jnp.concatenate([hi, lo], axis=0), w[0, t])
    return both[:n] + both[n:] + dot(hi, w[1, t])


def mul2(x, w, t):
    n = x.shape[0]
    hi, lo = split(x)
    both = dot(jnp.concatenate([hi, lo], axis=0), w[t])
    return both[:n] + both[n:]


def full(x, w, mul):
    x1, x2 = x[:, : 2 * H], x[:, 2 * H :]
    return jnp.concatenate([mul(x1, w, 0) + mul(x2, w, 1), mul(x2, w, 2)], axis=1)


def kernel(
    ndom, nx, nz, ainv, coup, src, out,
    loc, ez, oz, ex, ox, ed, od, sd, sx, wm, we, wt, wex, wd, wh, inj, fin,
    zs, zr, xs, xr, ds, dr, xds, xdr, zds, zdr,
):
    dom, run = lax.axis_index("dom"), lax.axis_index("run")
    x, z = run // nz, run % nz
    last_z, last_x = z == nz - 1, x == nx - 1

    def at(d, xx, zz):
        return (d, xx * nz + zz)

    z_up, z_dn = at(dom, x, (z + 1) % nz), at(dom, x, (z + nz - 1) % nz)
    x_up, x_dn = at(dom, (x + 1) % nx, z), at(dom, (x + nx - 1) % nx, z)
    d_up, d_dn = at((dom + 1) % ndom, x, z), at((dom + ndom - 1) % ndom, x, z)

    barrier = pltpu.get_barrier_semaphore()
    for who in (z_up, z_dn, x_up, x_dn, d_up, d_dn):
        pl.semaphore_signal(barrier, inc=1, device_id=who, device_id_type=MESH)

    for s in range(2):
        ar, ai = ainv[0, s, 0], ainv[0, s, 1]
        cr, ci = coup[s, 0], coup[s, 1]
        hr = (dot(ai, ci) - dot(ar, cr)).astype(BF16).astype(F32)
        hi = (-(dot(ar, ci) + dot(ai, cr))).astype(BF16).astype(F32)
        for t, (i, j) in enumerate(((0, 0), (0, H), (H, H))):
            top = jnp.concatenate(
                [hr[i : i + H, j : j + H].T, hi[i : i + H, j : j + H].T], axis=1
            )
            put_tile(wh.at[s], t, top.astype(BF16))
        sr, si = src[0, s, 0], src[0, s, 1]
        pr = dot(ar, sr) - dot(ai, si)
        pi = dot(ar, si) + dot(ai, sr)
        for h in range(2):
            inj[s, :, 2 * h * H : (2 * h + 1) * H] = pr[h * H : (h + 1) * H].T
            inj[s, :, (2 * h + 1) * H : (2 * h + 2) * H] = pi[h * H : (h + 1) * H].T
    w1 = wh.at[1]
    a11 = dot(wh[0, 0, 0:H, :], w1[0])
    loc[A11_ROW : A11_ROW + H // 2, : 2 * H] = a11[: H // 2]
    loc[A11_ROW : A11_ROW + H // 2, 2 * H :] = a11[H // 2 :]
    x1, x2 = wh[0, 1, 0:H, :], wh[0, 2, 0:H, :]
    loc[0:H, : 2 * H] = dot(x1, w1[0]) + dot(x2, w1[1])
    loc[0:H, 2 * H :] = dot(x2, w1[2])
    loc[B_ROW:, :] = full(inj[0], w1, mul2) + inj[1]
    put_weights(wm, loc)

    pl.semaphore_wait(barrier, 6)

    def copy(src_ref, dst_ref, c, ssem, rsem, who, first=0):
        r = rows(c * R, R)
        rd = rows((c - first) * R, R)
        return pltpu.make_async_remote_copy(
            src_ref=src_ref.at[r], dst_ref=dst_ref.at[rd], send_sem=ssem, recv_sem=rsem,
            device_id=who, device_id_type=MESH,
        )

    def arrive(buf, rsem, c):
        r = rows(c * R, R)
        pltpu.make_async_remote_copy(
            src_ref=buf.at[r], dst_ref=buf.at[r], send_sem=zs.at[c], recv_sem=rsem.at[c],
            device_id=z_up, device_id_type=MESH,
        ).wait_recv()

    def each(lo, hi, body):
        def step(c, carry):
            body(c)
            return carry

        lax.fori_loop(lo, hi, step, 0)

    def chain(inp, outp, w, own_b, rsem, send, between):
        def a2(c):
            arrive(inp, rsem, c)
            outp[rows(c * R, R), :] = full(inp[rows(c * R, R), :], w, mul3)
            send(c)

        def a11_(c):
            arrive(inp, rsem, c)
            v = inp[rows(c * R, R), :]
            y = mul3(jnp.concatenate([v[:, : 2 * H], v[:, 2 * H :]], axis=0), w, 0)
            outp[rows(c * R, R), :] = jnp.concatenate([y[:R], y[R:]], axis=1)
            send(c)

        def bb(c):
            arrive(inp, rsem, c)
            r = rows(c * R, R)
            outp[r, :] = full(inp[r, :], w, mul3) + own_b[r, :]
            send(c)

        each(0, NA2, a2)
        each(A11_CH, B_CH, a11_)
        between()
        each(B_CH, NC, bb)

    def z_copy(c, src_ref):
        return copy(src_ref, ez, c, zs.at[c], zr.at[c], z_up)

    def zx_copy(c, src_ref):
        return copy(src_ref, ex, c, zs.at[c], xr.at[c], x_up)

    @pl.when(z == 0)
    def _():
        each(0, NC, lambda c: z_copy(c, loc).start())

    @pl.when(z > 0)
    def _():
        def send(c):
            @pl.when(jnp.logical_not(last_z))
            def _():
                z_copy(c, oz).start()

            @pl.when(jnp.logical_and(last_z, x == 0))
            def _():
                zx_copy(c, oz).start()

        def between():
            @pl.when(last_z)
            def _():
                put_weights(wt, oz)

        chain(ez, oz, wm, loc, zr, send, between)
        put_weights(we, ez)

    def x_copy(c):
        return copy(ox, ex, c, xs.at[c], xr.at[c], x_up)

    def xd_copy(c):
        return copy(ox, ed, c, xs.at[c], dr.at[c - B_CH], d_up, first=B_CH)

    first_out = jnp.logical_and(last_x, dom == 0)

    @pl.when(jnp.logical_and(last_z, x > 0))
    def _():
        def send(c):
            @pl.when(jnp.logical_not(last_x))
            def _():
                x_copy(c).start()

            @pl.when(jnp.logical_and(first_out, c >= B_CH))
            def _():
                xd_copy(c).start()

        def between():
            @pl.when(last_x)
            def _():
                put_weights(wd, ox)

        chain(ex, ox, wt, oz, xr, send, between)
        put_weights(wex, ex)

    def d_copy(c):
        return copy(od, ed, c, ds.at[c], dr.at[c], d_up)

    def spread(n, place, buf, ssem, rsem, up, dn):
        plus = (n - 1) // 2

        def up_copy(c):
            return copy(buf, buf, c, ssem.at[0, c], rsem.at[c], up)

        def dn_copy(c):
            return copy(buf, buf, c, ssem.at[1, c], rsem.at[c], dn)

        to_up = jnp.logical_or(place == n - 1, place < plus - 1) if plus else place < 0
        to_dn = place > plus

        def go(c, wait):
            @pl.when(to_up)
            def _():
                cp = up_copy(c)
                cp.wait_send() if wait else cp.start()

            @pl.when(to_dn)
            def _():
                cp = dn_copy(c)
                cp.wait_send() if wait else cp.start()

        return go

    x_go = spread(nx, x, sd, xds, xdr, x_up, x_dn)
    z_go = spread(nz, z, sx, zds, zdr, z_up, z_dn)

    @pl.when(jnp.logical_and(last_z, last_x))
    def _():
        @pl.when(dom == 0)
        def _():
            sd[...] = jnp.zeros_like(sd)

        def step(c):
            r = rows(c * R, R)

            @pl.when(dom > 0)
            def _():
                arrive(ed, dr, c)

                @pl.when(dom < ndom - 1)
                def _():
                    od[r, :] = full(ed[r, :], wd, mul3) + ox[rows(B_ROW + c * R, R), :]
                    d_copy(c).start()

                sd[r, :] = ed[r, :]

            x_go(c, False)

        each(0, NB, step)

    @pl.when(last_z)
    def _():
        def step(c):
            r = rows(c * R, R)

            @pl.when(jnp.logical_not(last_x))
            def _():
                arrive(sd, xdr, c)
                x_go(c, False)

            @pl.when(x == 0)
            def _():
                sx[r, :] = sd[r, :]

            @pl.when(x > 0)
            def _():
                sx[r, :] = full(sd[r, :], wex, mul3) + ex[rows(B_ROW + c * R, R), :]

            z_go(c, False)

        each(0, NB, step)

    def finish(c):
        r = rows(c * R, R)

        @pl.when(jnp.logical_not(last_z))
        def _():
            arrive(sx, zdr, c)
            z_go(c, False)

        @pl.when(z == 0)
        def _():
            fin[0, r, :] = sx[r, :]

        @pl.when(z > 0)
        def _():
            fin[0, r, :] = full(sx[r, :], we, mul3) + ez[rows(B_ROW + c * R, R), :]

        s0 = full(fin[0, r, :], wh.at[0], mul2) + inj[0, r, :]
        fin[0, r, :] = s0
        fin[1, r, :] = full(s0, wh.at[1], mul2) + inj[1, r, :]

    each(0, NB, finish)
    for s in range(2):
        for p in range(2):
            for h in range(2):
                k = (2 * h + p) * H
                out[0, s, p, h * H : (h + 1) * H, :] = fin[s, :, k : k + H].T

    @pl.when(z == 0)
    def _():
        each(0, NC, lambda c: z_copy(c, loc).wait_send())

    @pl.when(jnp.logical_and(z > 0, jnp.logical_not(last_z)))
    def _():
        each(0, NC, lambda c: z_copy(c, oz).wait_send())

    @pl.when(jnp.logical_and(last_z, x == 0))
    def _():
        each(0, NC, lambda c: zx_copy(c, oz).wait_send())

    @pl.when(jnp.logical_and(last_z, jnp.logical_and(x > 0, jnp.logical_not(last_x))))
    def _():
        each(0, NC, lambda c: x_copy(c).wait_send())

    @pl.when(jnp.logical_and(last_z, first_out))
    def _():
        each(B_CH, NC, lambda c: xd_copy(c).wait_send())

    @pl.when(jnp.logical_and(last_z, last_x))
    def _():
        @pl.when(jnp.logical_and(dom > 0, dom < ndom - 1))
        def _():
            each(0, NB, lambda c: d_copy(c).wait_send())

    @pl.when(last_z)
    def _():
        each(0, NB, lambda c: x_go(c, True))

    each(0, NB, lambda c: z_go(c, True))


def build(mesh, nx):
    ndom, nrun = mesh.shape["dom"], mesh.shape["run"]
    nz = nrun // nx

    def shards(ainv, coupling, source):
        big = pltpu.VMEM((ROWS, 4 * H), F32)
        half = pltpu.VMEM((H, 4 * H), F32)
        weights = pltpu.VMEM((2, 3, 2 * H, 2 * H), BF16)
        sem = pltpu.SemaphoreType.DMA

        def body(*refs):
            kernel(ndom, nx, nz, *refs)

        vm = pl.BlockSpec(memory_space=pltpu.VMEM)
        return pl.pallas_call(
            body,
            out_shape=jax.ShapeDtypeStruct(source.shape, F32),
            in_specs=[vm] * 3,
            out_specs=vm,
            scratch_shapes=[
                big, big, big, big, big,
                half, half, half, half,
                weights, weights, weights, weights, weights,
                pltpu.VMEM((2, 3, 2 * H, 2 * H), BF16),
                pltpu.VMEM((2, H, 4 * H), F32),
                pltpu.VMEM((2, H, 4 * H), F32),
                sem((NC,)), sem((NC,)), sem((NC,)), sem((NC,)), sem((NB,)), sem((NB,)),
                sem((2, NB)), sem((NB,)), sem((2, NB)), sem((NB,)),
            ],
            compiler_params=pltpu.CompilerParams(
                collective_id=0, has_side_effects=True, vmem_limit_bytes=48 * 1024 * 1024
            ),
            name="sweep",
        )(ainv, coupling, source)

    in_specs = (
        P(None, ("dom", "run"), None, None, None),
        P(("dom", "run"), None, None, None),
        P(None, ("dom", "run"), None, None, None),
    )
    out_specs = P(None, ("dom", "run"), None, None, None)
    return jax.shard_map(shards, mesh=mesh, in_specs=in_specs, out_specs=out_specs, check_vma=False)


def solution(mesh):
    return build(mesh, NX)
```

```python
import jax
import jax.numpy as jnp
from jax import lax
from jax.experimental import pallas as pl
from jax.experimental.pallas import tpu as pltpu
from jax.sharding import PartitionSpec as P

MESH = pl.DeviceIdType.MESH
F32 = jnp.float32
BF16 = jnp.bfloat16

NX = 4
H = 128
R = 16
NA2 = H // R
NA11 = H // 2 // R
NB = H // R
A11_ROW = H
B_ROW = H + H // 2
ROWS = B_ROW + H
A11_CH = NA2
B_CH = NA2 + NA11
NC = B_CH + NB


def dot(a, b):
    return lax.dot_general(a, b, (((1,), (0,)), ((), ())), preferred_element_type=F32)


def split(x):
    hi = x.astype(BF16)
    return hi, (x - hi.astype(F32)).astype(BF16)


def rows(start, size):
    return pl.ds(pl.multiple_of(start, 8), size)


def put_tile(w, t, top):
    w[t, 0:H, :] = top
    w[t, H : 2 * H, 0:H] = -top[:, H:]
    w[t, H : 2 * H, H:] = top[:, :H]


def put_weights(w, buf):
    def one(t, top):
        hi, lo = split(top)
        put_tile(w.at[0], t, hi)
        put_tile(w.at[1], t, lo)

    a11 = buf[A11_ROW : A11_ROW + H // 2, :]
    one(0, jnp.concatenate([a11[:, : 2 * H], a11[:, 2 * H :]], axis=0))
    one(1, buf[0:H, 0 : 2 * H])
    one(2, buf[0:H, 2 * H :])


def mul3(x, w, t):
    n = x.shape[0]
    hi, lo = split(x)
    both = dot(jnp.concatenate([hi, lo], axis=0), w[0, t])
    return both[:n] + both[n:] + dot(hi, w[1, t])


def mul2(x, w, t):
    n = x.shape[0]
    hi, lo = split(x)
    both = dot(jnp.concatenate([hi, lo], axis=0), w[t])
    return both[:n] + both[n:]


def full(x, w, mul):
    x1, x2 = x[:, : 2 * H], x[:, 2 * H :]
    return jnp.concatenate([mul(x1, w, 0) + mul(x2, w, 1), mul(x2, w, 2)], axis=1)


def kernel(
    ndom, nx, nz, ainv_in, coup_in, src_in, out,
    ainv, coup, src, in_sem, loc, ez, oz, ex, ox, ed, od, sd, sx, wm, we, wt, wex, wd, wh, inj, fin,
    zs, zr, xs, xr, ds, dr, xds, xdr, zds, zdr,
):
    loads = []
    for s in range(2):
        loads.append([
            pltpu.make_async_copy(ainv_in.at[0, s], ainv.at[s], in_sem.at[s, 0]),
            pltpu.make_async_copy(coup_in.at[s], coup.at[s], in_sem.at[s, 1]),
            pltpu.make_async_copy(src_in.at[0, s], src.at[s], in_sem.at[s, 2]),
        ])
        for load in loads[s]:
            load.start()
    dom, run = lax.axis_index("dom"), lax.axis_index("run")
    x, z = run // nz, run % nz
    last_z, last_x = z == nz - 1, x == nx - 1

    def at(d, xx, zz):
        return (d, xx * nz + zz)

    z_up, z_dn = at(dom, x, (z + 1) % nz), at(dom, x, (z + nz - 1) % nz)
    x_up, x_dn = at(dom, (x + 1) % nx, z), at(dom, (x + nx - 1) % nx, z)
    d_up, d_dn = at((dom + 1) % ndom, x, z), at((dom + ndom - 1) % ndom, x, z)

    barrier = pltpu.get_barrier_semaphore()
    for who in (z_up, z_dn, x_up, x_dn, d_up, d_dn):
        pl.semaphore_signal(barrier, inc=1, device_id=who, device_id_type=MESH)

    for s in range(2):
        for load in loads[s]:
            load.wait()
        ar, ai = ainv[s, 0], ainv[s, 1]
        cr, ci = coup[s, 0], coup[s, 1]
        hr = (dot(ai, ci) - dot(ar, cr)).astype(BF16).astype(F32)
        hi = (-(dot(ar, ci) + dot(ai, cr))).astype(BF16).astype(F32)
        for t, (i, j) in enumerate(((0, 0), (0, H), (H, H))):
            top = jnp.concatenate(
                [hr[i : i + H, j : j + H].T, hi[i : i + H, j : j + H].T], axis=1
            )
            put_tile(wh.at[s], t, top.astype(BF16))
        sr, si = src[s, 0], src[s, 1]
        pr = dot(ar, sr) - dot(ai, si)
        pi = dot(ar, si) + dot(ai, sr)
        for h in range(2):
            inj[s, :, 2 * h * H : (2 * h + 1) * H] = pr[h * H : (h + 1) * H].T
            inj[s, :, (2 * h + 1) * H : (2 * h + 2) * H] = pi[h * H : (h + 1) * H].T
    w1 = wh.at[1]
    a11 = dot(wh[0, 0, 0:H, :], w1[0])
    loc[A11_ROW : A11_ROW + H // 2, : 2 * H] = a11[: H // 2]
    loc[A11_ROW : A11_ROW + H // 2, 2 * H :] = a11[H // 2 :]
    x1, x2 = wh[0, 1, 0:H, :], wh[0, 2, 0:H, :]
    loc[0:H, : 2 * H] = dot(x1, w1[0]) + dot(x2, w1[1])
    loc[0:H, 2 * H :] = dot(x2, w1[2])
    loc[B_ROW:, :] = full(inj[0], w1, mul2) + inj[1]
    put_weights(wm, loc)

    pl.semaphore_wait(barrier, 6)

    def copy(src_ref, dst_ref, c, ssem, rsem, who, first=0):
        r = rows(c * R, R)
        rd = rows((c - first) * R, R)
        return pltpu.make_async_remote_copy(
            src_ref=src_ref.at[r], dst_ref=dst_ref.at[rd], send_sem=ssem, recv_sem=rsem,
            device_id=who, device_id_type=MESH,
        )

    def arrive(buf, rsem, c):
        r = rows(c * R, R)
        pltpu.make_async_remote_copy(
            src_ref=buf.at[r], dst_ref=buf.at[r], send_sem=zs.at[c], recv_sem=rsem.at[c],
            device_id=z_up, device_id_type=MESH,
        ).wait_recv()

    def each(lo, hi, body):
        def step(c, carry):
            body(c)
            return carry

        lax.fori_loop(lo, hi, step, 0)

    def chain(inp, outp, w, own_b, rsem, send, between):
        def a2(c):
            arrive(inp, rsem, c)
            outp[rows(c * R, R), :] = full(inp[rows(c * R, R), :], w, mul3)
            send(c)

        def a11_(c):
            arrive(inp, rsem, c)
            v = inp[rows(c * R, R), :]
            y = mul3(jnp.concatenate([v[:, : 2 * H], v[:, 2 * H :]], axis=0), w, 0)
            outp[rows(c * R, R), :] = jnp.concatenate([y[:R], y[R:]], axis=1)
            send(c)

        def bb(c):
            arrive(inp, rsem, c)
            r = rows(c * R, R)
            outp[r, :] = full(inp[r, :], w, mul3) + own_b[r, :]
            send(c)

        each(0, NA2, a2)
        each(A11_CH, B_CH, a11_)
        between()
        each(B_CH, NC, bb)

    def z_copy(c, src_ref):
        return copy(src_ref, ez, c, zs.at[c], zr.at[c], z_up)

    def zx_copy(c, src_ref):
        return copy(src_ref, ex, c, zs.at[c], xr.at[c], x_up)

    @pl.when(z == 0)
    def _():
        each(0, NC, lambda c: z_copy(c, loc).start())

    @pl.when(z > 0)
    def _():
        def send(c):
            @pl.when(jnp.logical_not(last_z))
            def _():
                z_copy(c, oz).start()

            @pl.when(jnp.logical_and(last_z, x == 0))
            def _():
                zx_copy(c, oz).start()

        def between():
            @pl.when(last_z)
            def _():
                put_weights(wt, oz)

        chain(ez, oz, wm, loc, zr, send, between)
        put_weights(we, ez)

    def x_copy(c):
        return copy(ox, ex, c, xs.at[c], xr.at[c], x_up)

    def xd_copy(c):
        return copy(ox, ed, c, xs.at[c], dr.at[c - B_CH], d_up, first=B_CH)

    first_out = jnp.logical_and(last_x, dom == 0)

    @pl.when(jnp.logical_and(last_z, x > 0))
    def _():
        def send(c):
            @pl.when(jnp.logical_not(last_x))
            def _():
                x_copy(c).start()

            @pl.when(jnp.logical_and(first_out, c >= B_CH))
            def _():
                xd_copy(c).start()

        def between():
            @pl.when(last_x)
            def _():
                put_weights(wd, ox)

        chain(ex, ox, wt, oz, xr, send, between)
        put_weights(wex, ex)

    def d_copy(c):
        return copy(od, ed, c, ds.at[c], dr.at[c], d_up)

    def spread(n, place, buf, ssem, rsem, up, dn):
        plus = (n - 1) // 2

        def up_copy(c):
            return copy(buf, buf, c, ssem.at[0, c], rsem.at[c], up)

        def dn_copy(c):
            return copy(buf, buf, c, ssem.at[1, c], rsem.at[c], dn)

        to_up = jnp.logical_or(place == n - 1, place < plus - 1) if plus else place < 0
        to_dn = place > plus

        def go(c, wait):
            @pl.when(to_up)
            def _():
                cp = up_copy(c)
                cp.wait_send() if wait else cp.start()

            @pl.when(to_dn)
            def _():
                cp = dn_copy(c)
                cp.wait_send() if wait else cp.start()

        return go

    x_go = spread(nx, x, sd, xds, xdr, x_up, x_dn)
    z_go = spread(nz, z, sx, zds, zdr, z_up, z_dn)

    @pl.when(jnp.logical_and(last_z, last_x))
    def _():
        @pl.when(dom == 0)
        def _():
            sd[...] = jnp.zeros_like(sd)

        def step(c):
            r = rows(c * R, R)

            @pl.when(dom > 0)
            def _():
                arrive(ed, dr, c)

                @pl.when(dom < ndom - 1)
                def _():
                    od[r, :] = full(ed[r, :], wd, mul3) + ox[rows(B_ROW + c * R, R), :]
                    d_copy(c).start()

                sd[r, :] = ed[r, :]

            x_go(c, False)

        each(0, NB, step)

    @pl.when(last_z)
    def _():
        def step(c):
            r = rows(c * R, R)

            @pl.when(jnp.logical_not(last_x))
            def _():
                arrive(sd, xdr, c)
                x_go(c, False)

            @pl.when(x == 0)
            def _():
                sx[r, :] = sd[r, :]

            @pl.when(x > 0)
            def _():
                sx[r, :] = full(sd[r, :], wex, mul3) + ex[rows(B_ROW + c * R, R), :]

            z_go(c, False)

        each(0, NB, step)

    def finish(c):
        r = rows(c * R, R)

        @pl.when(jnp.logical_not(last_z))
        def _():
            arrive(sx, zdr, c)
            z_go(c, False)

        @pl.when(z == 0)
        def _():
            fin[0, r, :] = sx[r, :]

        @pl.when(z > 0)
        def _():
            fin[0, r, :] = full(sx[r, :], we, mul3) + ez[rows(B_ROW + c * R, R), :]

        s0 = full(fin[0, r, :], wh.at[0], mul2) + inj[0, r, :]
        fin[0, r, :] = s0
        fin[1, r, :] = full(s0, wh.at[1], mul2) + inj[1, r, :]

    each(0, NB, finish)
    for s in range(2):
        for p in range(2):
            for h in range(2):
                k = (2 * h + p) * H
                out[0, s, p, h * H : (h + 1) * H, :] = fin[s, :, k : k + H].T

    @pl.when(z == 0)
    def _():
        each(0, NC, lambda c: z_copy(c, loc).wait_send())

    @pl.when(jnp.logical_and(z > 0, jnp.logical_not(last_z)))
    def _():
        each(0, NC, lambda c: z_copy(c, oz).wait_send())

    @pl.when(jnp.logical_and(last_z, x == 0))
    def _():
        each(0, NC, lambda c: zx_copy(c, oz).wait_send())

    @pl.when(jnp.logical_and(last_z, jnp.logical_and(x > 0, jnp.logical_not(last_x))))
    def _():
        each(0, NC, lambda c: x_copy(c).wait_send())

    @pl.when(jnp.logical_and(last_z, first_out))
    def _():
        each(B_CH, NC, lambda c: xd_copy(c).wait_send())

    @pl.when(jnp.logical_and(last_z, last_x))
    def _():
        @pl.when(jnp.logical_and(dom > 0, dom < ndom - 1))
        def _():
            each(0, NB, lambda c: d_copy(c).wait_send())

    @pl.when(last_z)
    def _():
        each(0, NB, lambda c: x_go(c, True))

    each(0, NB, lambda c: z_go(c, True))


def build(mesh, nx):
    ndom, nrun = mesh.shape["dom"], mesh.shape["run"]
    nz = nrun // nx

    def shards(ainv, coupling, source):
        big = pltpu.VMEM((ROWS, 4 * H), F32)
        half = pltpu.VMEM((H, 4 * H), F32)
        weights = pltpu.VMEM((2, 3, 2 * H, 2 * H), BF16)
        sem = pltpu.SemaphoreType.DMA

        def body(*refs):
            kernel(ndom, nx, nz, *refs)

        vm = pl.BlockSpec(memory_space=pltpu.VMEM)
        return pl.pallas_call(
            body,
            out_shape=jax.ShapeDtypeStruct(source.shape, F32),
            in_specs=[pl.BlockSpec(memory_space=pl.ANY)] * 3,
            out_specs=vm,
            scratch_shapes=[
                pltpu.VMEM((2, 2, 2 * H, 2 * H), BF16),
                pltpu.VMEM((2, 2, 2 * H, 2 * H), BF16),
                pltpu.VMEM((2, 2, 2 * H, H), BF16),
                sem((2, 3)),
                big, big, big, big, big,
                half, half, half, half,
                weights, weights, weights, weights, weights,
                pltpu.VMEM((2, 3, 2 * H, 2 * H), BF16),
                pltpu.VMEM((2, H, 4 * H), F32),
                pltpu.VMEM((2, H, 4 * H), F32),
                sem((NC,)), sem((NC,)), sem((NC,)), sem((NC,)), sem((NB,)), sem((NB,)),
                sem((2, NB)), sem((NB,)), sem((2, NB)), sem((NB,)),
            ],
            compiler_params=pltpu.CompilerParams(
                collective_id=0, has_side_effects=True, vmem_limit_bytes=67043328
            ),
            name="sweep",
        )(ainv, coupling, source)

    in_specs = (
        P(None, ("dom", "run"), None, None, None),
        P(("dom", "run"), None, None, None),
        P(None, ("dom", "run"), None, None, None),
    )
    out_specs = P(None, ("dom", "run"), None, None, None)
    return jax.shard_map(shards, mesh=mesh, in_specs=in_specs, out_specs=out_specs, check_vma=False)


def solution(mesh):
    return build(mesh, NX)
```

```python
import jax
import jax.numpy as jnp
from jax import lax
from jax.experimental import pallas as pl
from jax.experimental.pallas import tpu as pltpu
from jax.sharding import PartitionSpec as P

MESH = pl.DeviceIdType.MESH
F32 = jnp.float32
BF16 = jnp.bfloat16

NX = 4
H = 128
R = 16
NA2 = H // R
NA11 = H // 2 // R
NB = H // R
A11_ROW = H
B_ROW = H + H // 2
ROWS = B_ROW + H
A11_CH = NA2
B_CH = NA2 + NA11
NC = B_CH + NB


def dot(a, b):
    return lax.dot_general(a, b, (((1,), (0,)), ((), ())), preferred_element_type=F32)


def split(x):
    hi = x.astype(BF16)
    return hi, (x - hi.astype(F32)).astype(BF16)


def rows(start, size):
    return pl.ds(pl.multiple_of(start, 8), size)


def put_tile(w, t, top):
    w[t, 0:H, :] = top
    w[t, H : 2 * H, 0:H] = -top[:, H:]
    w[t, H : 2 * H, H:] = top[:, :H]


def put_pair(w, t, top):
    hi, lo = split(top)
    put_tile(w.at[0], t, hi)
    put_tile(w.at[1], t, lo)


def unstack(v):
    return jnp.concatenate([v[:, : 2 * H], v[:, 2 * H :]], axis=0)


def stack(y):
    n = y.shape[0] // 2
    return jnp.concatenate([y[:n], y[n:]], axis=1)


def packed(buf):
    return unstack(buf[A11_ROW:B_ROW, :])


def put_weights(w, buf):
    put_pair(w, 0, packed(buf))
    put_pair(w, 1, buf[0:H, 0 : 2 * H])
    put_pair(w, 2, buf[0:H, 2 * H :])


def put_weights_n(w, wb, buf):
    put_pair(w, 0, buf[0:H, 0 : 2 * H])
    put_pair(w, 1, buf[0:H, 2 * H :])
    put_pair(w, 2, packed(buf))
    put_pair(wb, 0, buf[B_ROW:, 0 : 2 * H])
    put_pair(wb, 1, buf[B_ROW:, 2 * H :])


def flip(v):
    return jnp.concatenate([v[:, k : k + H].T for k in range(0, v.shape[1], H)], axis=1)


def turn_a(src, dst, to_plain):
    first, second, third = src[0:H, 0 : 2 * H], src[0:H, 2 * H :], packed(src)
    order = (third, first, second) if to_plain else (second, third, first)
    dst[0:H, 0 : 2 * H] = flip(order[0])
    dst[0:H, 2 * H :] = flip(order[1])
    dst[A11_ROW:B_ROW, :] = stack(flip(order[2]))


def turn_b(src, dst):
    dst[B_ROW:, :] = flip(src[B_ROW:, :])


def mul3(x, w, t):
    n = x.shape[0]
    hi, lo = split(x)
    both = dot(jnp.concatenate([hi, lo], axis=0), w[0, t])
    return both[:n] + both[n:] + dot(hi, w[1, t])


def mul2(x, w, t):
    n = x.shape[0]
    hi, lo = split(x)
    both = dot(jnp.concatenate([hi, lo], axis=0), w[t])
    return both[:n] + both[n:]


def full(x, w, mul):
    x1, x2 = x[:, : 2 * H], x[:, 2 * H :]
    return jnp.concatenate([mul(x1, w, 0) + mul(x2, w, 1), mul(x2, w, 2)], axis=1)


def kernel(
    ndom, nx, nz, ainv_in, coup_in, src_in, out,
    ainv, coup, src, in_sem,
    loc, ez, oz, ex, ox, es, os, nloc, ep, op, ed, od, sd, sx,
    wm, we, wt, wex, wd, wn, wp, wep, wb, wh, inj, fin,
    zs, zr, xs, xr, ss, sr, pr, ds, dr, fs, xds, xdr, zds, zdr,
):
    loads = []
    for s in range(2):
        loads.append([
            pltpu.make_async_copy(ainv_in.at[0, s], ainv.at[s], in_sem.at[s, 0]),
            pltpu.make_async_copy(coup_in.at[s], coup.at[s], in_sem.at[s, 1]),
            pltpu.make_async_copy(src_in.at[0, s], src.at[s], in_sem.at[s, 2]),
        ])
        for load in loads[s]:
            load.start()
    dom, run = lax.axis_index("dom"), lax.axis_index("run")
    x, z = run // nz, run % nz
    y, odd = dom // 2, dom % 2 == 1
    even = jnp.logical_not(odd)
    ny = ndom // 2
    gate = jnp.where(odd, z == 0, z == nz - 1)
    last_x = x == nx - 1
    both = jnp.logical_and

    def at(d, xx, zz):
        return (d, xx * nz + zz)

    z_up, z_dn = at(dom, x, (z + 1) % nz), at(dom, x, (z + nz - 1) % nz)
    x_up, x_dn = at(dom, (x + 1) % nx, z), at(dom, (x + nx - 1) % nx, z)
    d_up, d_dn = at((dom + 2) % ndom, x, z), at((dom + ndom - 2) % ndom, x, z)
    twin = at(dom + 1 - 2 * (dom % 2), x, jnp.where(odd, z + nz - 1, z + 1) % nz)

    barrier = pltpu.get_barrier_semaphore()
    greet = (z_up, z_dn, x_up, x_dn, twin) + ((d_up, d_dn) if ny > 1 else ())
    for who in greet:
        pl.semaphore_signal(barrier, inc=1, device_id=who, device_id_type=MESH)

    for s in range(2):
        for load in loads[s]:
            load.wait()
        ar, ai = ainv[s, 0], ainv[s, 1]
        cr, ci = coup[s, 0], coup[s, 1]
        hr = (dot(ai, ci) - dot(ar, cr)).astype(BF16).astype(F32)
        hi = (-(dot(ar, ci) + dot(ai, cr))).astype(BF16).astype(F32)
        for t, (i, j) in enumerate(((0, 0), (0, H), (H, H))):
            top = jnp.concatenate(
                [hr[i : i + H, j : j + H].T, hi[i : i + H, j : j + H].T], axis=1
            )
            put_tile(wh.at[s], t, top.astype(BF16))
        sr_, si_ = src[s, 0], src[s, 1]
        pr_ = dot(ar, sr_) - dot(ai, si_)
        pi_ = dot(ar, si_) + dot(ai, sr_)
        for h in range(2):
            inj[s, :, 2 * h * H : (2 * h + 1) * H] = pr_[h * H : (h + 1) * H].T
            inj[s, :, (2 * h + 1) * H : (2 * h + 2) * H] = pi_[h * H : (h + 1) * H].T
    w1 = wh.at[1]
    loc[A11_ROW:B_ROW, :] = stack(dot(wh[0, 0, 0:H, :], w1[0]))
    x1, x2 = wh[0, 1, 0:H, :], wh[0, 2, 0:H, :]
    loc[0:H, : 2 * H] = dot(x1, w1[0]) + dot(x2, w1[1])
    loc[0:H, 2 * H :] = dot(x2, w1[2])
    loc[B_ROW:, :] = full(inj[0], w1, mul2) + inj[1]
    put_weights(wm, loc)

    @pl.when(odd)
    def _():
        turn_a(loc, nloc, True)
        turn_b(loc, nloc)
        put_weights_n(wn, wb, nloc)

    pl.semaphore_wait(barrier, len(greet))

    def copy(src_ref, dst_ref, c, ssem, rsem, who, s_off=0):
        return pltpu.make_async_remote_copy(
            src_ref=src_ref.at[rows((c + s_off) * R, R)], dst_ref=dst_ref.at[rows(c * R, R)],
            send_sem=ssem, recv_sem=rsem, device_id=who, device_id_type=MESH,
        )

    def sent(buf, ssem):
        pltpu.make_async_remote_copy(
            src_ref=buf, dst_ref=buf, send_sem=ssem, recv_sem=zr.at[0],
            device_id=z_up, device_id_type=MESH,
        ).wait_send()

    def arrive(buf, rsem, c):
        copy(buf, buf, c, zs, rsem.at[c], z_up).wait_recv()

    def each(lo, hi, body):
        def step(c, carry):
            body(c)
            return carry

        lax.fori_loop(lo, hi, step, 0)

    def when(cond, body):
        pl.when(cond)(body)

    def chain_a(inp, outp, w, rsem, send):
        def a2(c):
            arrive(inp, rsem, c)
            outp[rows(c * R, R), :] = full(inp[rows(c * R, R), :], w, mul3)
            send(c)

        def a11(c):
            arrive(inp, rsem, c)
            outp[rows(c * R, R), :] = stack(mul3(unstack(inp[rows(c * R, R), :]), w, 0))
            send(c)

        each(0, NA2, a2)
        each(A11_CH, B_CH, a11)

    def chain_b(inp, outp, w, own, rsem, send):
        def bb(c):
            arrive(inp, rsem, c)
            r = rows(c * R, R)
            outp[r, :] = full(inp[r, :], w, mul3) + own[r, :]
            send(c)

        each(B_CH, NC, bb)

    def back_a(inp, outp, send):
        def top(c):
            arrive(inp, sr, c)
            v = inp[rows(c * R, R), :]
            v1, v2 = v[:, : 2 * H], v[:, 2 * H :]
            outp[rows(c * R, R), :] = jnp.concatenate(
                [mul3(v1, wn, 0), mul3(v1, wn, 1) + mul3(v2, wn, 2)], axis=1
            )
            send(c)

        def low(c):
            arrive(inp, sr, c)
            outp[rows(c * R, R), :] = stack(mul3(unstack(inp[rows(c * R, R), :]), wn, 2))
            send(c)

        each(0, NA2, top)
        each(A11_CH, B_CH, low)

    def back_b(inp, outp, send):
        def bb(q):
            for half in range(2):
                k = q + half * (NB // 2)
                c = B_CH + k
                arrive(inp, sr, c)
                v = inp[rows(k * R, R), :]
                low = inp[rows(A11_ROW + q * R, R), half * 2 * H : (half + 1) * 2 * H]
                y1 = mul3(v[:, : 2 * H], wb, 0) + mul3(v[:, 2 * H :], wb, 1)
                y2 = mul3(low, wb, 1)
                r = rows(c * R, R)
                outp[r, :] = jnp.concatenate([y1, y2], axis=1) + inp[r, :]
                send(c)

        each(0, NB // 2, bb)

    def z_copy(c, src_ref):
        return copy(src_ref, ez, c, zs, zr.at[c], z_up)

    def s_copy(c, src_ref):
        return copy(src_ref, es, c, ss, sr.at[c], z_dn)

    def x_copy(c, src_ref):
        return copy(src_ref, ex, c, xs, xr.at[c], x_up)

    def p_copy(c):
        return copy(ox, ep, c, xs, pr.at[c], twin)

    def nothing(c):
        pass

    @pl.when(both(even, z == 0))
    def _():
        each(0, NC, lambda c: z_copy(c, loc).start())

    @pl.when(both(even, z > 0))
    def _():
        def send(c):
            when(jnp.logical_not(gate), lambda: z_copy(c, oz).start())
            when(both(gate, x == 0), lambda: x_copy(c, oz).start())

        chain_a(ez, oz, wm, zr, send)
        when(both(gate, x > 0), lambda: put_weights(wt, oz))
        chain_b(ez, oz, wm, loc, zr, send)

    @pl.when(both(odd, z == nz - 1))
    def _():
        each(0, NC, lambda c: s_copy(c, nloc).start())

    @pl.when(both(odd, jnp.logical_and(z > 0, z < nz - 1)))
    def _():
        def send(c):
            s_copy(c, os).start()

        back_a(es, os, send)
        back_b(es, os, send)

    @pl.when(both(odd, z == 0))
    def _():
        def send(c):
            @pl.when(c == 0)
            def _():
                each(0, NC, lambda k: z_copy(k, loc).start())

        back_a(es, os, send)
        turn_a(os, oz, False)
        when(x == 0, lambda: each(0, B_CH, lambda c: x_copy(c, oz).start()))
        when(x > 0, lambda: put_weights(wt, oz))
        back_b(es, os, nothing)
        turn_b(os, oz)
        when(x == 0, lambda: each(B_CH, NC, lambda c: x_copy(c, oz).start()))

    p_all = y > 0

    @pl.when(both(gate, x > 0))
    def _():
        def send(c):
            when(jnp.logical_not(last_x), lambda: x_copy(c, ox).start())
            when(
                both(both(last_x, even), jnp.logical_or(p_all, c >= B_CH)),
                lambda: p_copy(c).start(),
            )

        chain_a(ex, ox, wt, xr, send)
        when(both(last_x, odd), lambda: put_weights(wd, ox))
        chain_b(ex, ox, wt, oz, xr, send)
        put_weights(wex, ex)

    @pl.when(both(odd, z > 0))
    def _():
        @pl.when(z < nz - 1)
        def _():
            def send(c):
                z_copy(c, oz).start()

            chain_a(ez, oz, wm, zr, send)
            chain_b(ez, oz, wm, loc, zr, send)

        when(z == nz - 1, lambda: each(0, NC, lambda c: arrive(ez, zr, c)))

    when(z > 0, lambda: put_weights(we, ez))

    def spread(n, place, buf, ssem, rsem, up, dn):
        plus = (n - 1) // 2

        def up_copy(c):
            return copy(buf, buf, c, ssem.at[0], rsem.at[c], up)

        def dn_copy(c):
            return copy(buf, buf, c, ssem.at[1], rsem.at[c], dn)

        to_up = jnp.logical_or(place == n - 1, place < plus - 1) if plus else place < 0
        to_dn = place > plus

        def go(c):
            when(to_up, lambda: up_copy(c).start())
            when(to_dn, lambda: dn_copy(c).start())

        def drain():
            when(to_up, lambda: sent(buf, ssem.at[0]))
            when(to_dn, lambda: sent(buf, ssem.at[1]))

        return go, drain

    x_go, x_drain = spread(nx, x, sd, xds, xdr, x_up, x_dn)
    z_place = jnp.where(odd, z + nz - 1, z) % nz
    z_go, z_drain = spread(nz, z_place, sx, zds, zdr, z_up, z_dn)

    def first_copy(c):
        return copy(op, ed, c, ds, dr.at[c], d_up, s_off=B_CH)

    def d_copy(c):
        return copy(od, ed, c, ds, dr.at[c], d_up)

    def f_copy(c):
        return copy(ed, sd, c, fs, xdr.at[c], twin)

    head = both(gate, last_x)
    odd_head = both(head, odd)

    @pl.when(odd_head)
    def _():
        if ny > 1:
            @pl.when(both(y > 0, y < ny - 1))
            def _():
                chain_a(ep, op, wd, pr, nothing)
                put_weights(wp, op)

            when(y == ny - 1, lambda: each(0, B_CH, lambda c: arrive(ep, pr, c)))
            when(y > 0, lambda: put_weights(wep, ep))

        def pair(c):
            b = rows(B_ROW + c * R, R)
            arrive(ep, pr, c + B_CH)

            @pl.when(y < ny - 1)
            def _():
                op[b, :] = full(ep[b, :], wd, mul3) + ox[b, :]
                when(y == 0, lambda: first_copy(c).start())

            @pl.when(y == 0)
            def _():
                sd[rows(c * R, R), :] = ep[b, :]
                x_go(c)

        each(0, NB, pair)

        if ny > 1:
            def step(c):
                r, b = rows(c * R, R), rows(B_ROW + c * R, R)
                arrive(ed, dr, c)

                @pl.when(y < ny - 1)
                def _():
                    od[r, :] = full(ed[r, :], wp, mul3) + op[b, :]
                    d_copy(c).start()

                f_copy(c).start()
                sd[r, :] = full(ed[r, :], wep, mul3) + ep[b, :]
                x_go(c)

            when(y > 0, lambda: each(0, NB, step))

    @pl.when(gate)
    def _():
        @pl.when(both(last_x, dom == 0))
        def _():
            sd[...] = jnp.zeros_like(sd)

        def step(c):
            r = rows(c * R, R)

            @pl.when(jnp.logical_not(odd_head))
            def _():
                when(jnp.logical_not(both(last_x, dom == 0)), lambda: arrive(sd, xdr, c))
                x_go(c)

            @pl.when(x == 0)
            def _():
                sx[r, :] = sd[r, :]

            @pl.when(x > 0)
            def _():
                sx[r, :] = full(sd[r, :], wex, mul3) + ex[rows(B_ROW + c * R, R), :]

            z_go(c)

        each(0, NB, step)

    def finish(start, size):
        r = rows(start, size)

        @pl.when(z == 0)
        def _():
            fin[0, r, :] = sx[r, :]

        @pl.when(z > 0)
        def _():
            fin[0, r, :] = full(sx[r, :], we, mul3) + ez[rows(B_ROW + start, size), :]

        s0 = full(fin[0, r, :], wh.at[0], mul2) + inj[0, r, :]
        fin[0, r, :] = s0
        fin[1, r, :] = full(s0, wh.at[1], mul2) + inj[1, r, :]

    @pl.when(jnp.logical_not(gate))
    def _():
        def pass_on(c):
            arrive(sx, zdr, c)
            z_go(c)

        each(0, NB, pass_on)

    each(0, 2, lambda c: finish(c * (H // 2), H // 2))

    for s in range(2):
        for p in range(2):
            for h in range(2):
                k = (2 * h + p) * H
                out[0, s, p, h * H : (h + 1) * H, :] = fin[s, :, k : k + H].T

    when(jnp.logical_or(z == 0, z < nz - 1), lambda: sent(ez, zs))
    when(both(odd, z > 0), lambda: sent(es, ss))
    first_pair = both(both(head, even), jnp.logical_not(p_all))
    when(both(gate, jnp.logical_not(both(last_x, jnp.logical_or(odd, first_pair)))), lambda: sent(ex, xs))
    when(first_pair, lambda: sent(ex.at[B_ROW:ROWS], xs))
    if ny > 1:
        when(both(odd_head, y < ny - 1), lambda: sent(ed, ds))
        when(both(odd_head, y > 0), lambda: sent(ed, fs))
    when(gate, x_drain)
    z_drain()


def build(mesh, nx):
    ndom, nrun = mesh.shape["dom"], mesh.shape["run"]
    nz = nrun // nx

    def shards(ainv, coupling, source):
        big = pltpu.VMEM((ROWS, 4 * H), F32)
        half = pltpu.VMEM((H, 4 * H), F32)
        weights = pltpu.VMEM((2, 3, 2 * H, 2 * H), BF16)
        sem = pltpu.SemaphoreType.DMA

        def body(*refs):
            kernel(ndom, nx, nz, *refs)

        vm = pl.BlockSpec(memory_space=pltpu.VMEM)
        return pl.pallas_call(
            body,
            out_shape=jax.ShapeDtypeStruct(source.shape, F32),
            in_specs=[pl.BlockSpec(memory_space=pltpu.HBM)] * 3,
            out_specs=vm,
            scratch_shapes=[
                pltpu.VMEM((2, 2, 2 * H, 2 * H), BF16),
                pltpu.VMEM((2, 2, 2 * H, 2 * H), BF16),
                pltpu.VMEM((2, 2, 2 * H, H), BF16),
                sem((2, 3)),
                big, big, big, big, big, big, big, big, big, big,
                half, half, half, half,
                weights, weights, weights, weights, weights, weights, weights, weights,
                pltpu.VMEM((2, 2, 2 * H, 2 * H), BF16),
                pltpu.VMEM((2, 3, 2 * H, 2 * H), BF16),
                pltpu.VMEM((2, H, 4 * H), F32),
                pltpu.VMEM((2, H, 4 * H), F32),
                sem, sem((NC,)), sem, sem((NC,)), sem, sem((NC,)), sem((NC,)),
                sem, sem((NB,)), sem,
                sem((2,)), sem((NB,)), sem((2,)), sem((NB,)),
            ],
            compiler_params=pltpu.CompilerParams(
                collective_id=0, has_side_effects=True, vmem_limit_bytes=67043328
            ),
            name="sweep",
        )(ainv, coupling, source)

    in_specs = (
        P(None, ("dom", "run"), None, None, None),
        P(("dom", "run"), None, None, None),
        P(None, ("dom", "run"), None, None, None),
    )
    out_specs = P(None, ("dom", "run"), None, None, None)
    return jax.shard_map(shards, mesh=mesh, in_specs=in_specs, out_specs=out_specs, check_vma=False)


def solution(mesh):
    return build(mesh, NX)
```

```python
import jax
import jax.numpy as jnp
from jax import lax
from jax.experimental import pallas as pl
from jax.experimental.pallas import tpu as pltpu
from jax.sharding import PartitionSpec as P

MESH = pl.DeviceIdType.MESH
F32 = jnp.float32
BF16 = jnp.bfloat16

NX = 4
H = 128
R = 16
NA2 = H // R
NA11 = H // 2 // R
NB = H // R
A11_ROW = H
B_ROW = H + H // 2
ROWS = B_ROW + H
A11_CH = NA2
B_CH = NA2 + NA11
NC = B_CH + NB


def dot(a, b):
    return lax.dot_general(a, b, (((1,), (0,)), ((), ())), preferred_element_type=F32)


def split(x):
    hi = x.astype(BF16)
    return hi, (x - hi.astype(F32)).astype(BF16)


def rows(start, size):
    return pl.ds(pl.multiple_of(start, 8), size)


def put_tile(w, t, top):
    k = t * 2 * H
    w[k : k + H, :] = top
    w[k + H : k + 2 * H, 0:H] = -top[:, H:]
    w[k + H : k + 2 * H, H:] = top[:, :H]


def tile(t, n=1):
    return slice(t * 2 * H, (t + n) * 2 * H)


def put_pair(w, t, top):
    hi, lo = split(top)
    put_tile(w.at[0], t, hi)
    put_tile(w.at[1], t, lo)


def unstack(v):
    return jnp.concatenate([v[:, : 2 * H], v[:, 2 * H :]], axis=0)


def stack(y):
    n = y.shape[0] // 2
    return jnp.concatenate([y[:n], y[n:]], axis=1)


def packed(buf):
    return unstack(buf[A11_ROW:B_ROW, :])


def put_weights(w, buf):
    put_pair(w, 0, packed(buf))
    put_pair(w, 1, buf[0:H, 0 : 2 * H])
    put_pair(w, 2, buf[0:H, 2 * H :])


def put_weights_n(w, wb, buf):
    put_pair(w, 0, buf[0:H, 0 : 2 * H])
    put_pair(w, 1, buf[0:H, 2 * H :])
    put_pair(w, 2, packed(buf))
    put_pair(wb, 0, buf[B_ROW:, 0 : 2 * H])
    put_pair(wb, 1, buf[B_ROW:, 2 * H :])


def flip(v):
    return jnp.concatenate([v[:, k : k + H].T for k in range(0, v.shape[1], H)], axis=1)


def turn_a(src, dst, to_plain):
    first, second, third = src[0:H, 0 : 2 * H], src[0:H, 2 * H :], packed(src)
    order = (third, first, second) if to_plain else (second, third, first)
    dst[0:H, 0 : 2 * H] = flip(order[0])
    dst[0:H, 2 * H :] = flip(order[1])
    dst[A11_ROW:B_ROW, :] = stack(flip(order[2]))


def turn_b(src, dst):
    dst[B_ROW:, :] = flip(src[B_ROW:, :])


def mul3(x, w, t, k=1):
    n = x.shape[0]
    hi, lo = split(x)
    both = dot(jnp.concatenate([hi, lo], axis=0), w[0, tile(t, k), :])
    return both[:n] + both[n:] + dot(hi, w[1, tile(t, k), :])


def mul2(x, w, t, k=1):
    n = x.shape[0]
    hi, lo = split(x)
    both = dot(jnp.concatenate([hi, lo], axis=0), w[tile(t, k), :])
    return both[:n] + both[n:]


def full(x, w, mul):
    return jnp.concatenate([mul(x, w, 0, 2), mul(x[:, 2 * H :], w, 2)], axis=1)


def kernel(
    ndom, nx, nz, ainv_in, coup_in, src_in, out,
    ainv, coup, src, in_sem,
    loc, ez, oz, ex, ox, es, os, nloc, ep, op, ed, od, o1, sd, sx,
    wm, we, wt, wex, wd, wn, wp, wep, wb, wh, inj, fin,
    zs, zr, xs, xr, ss, sr, pr, ds, dr, fs, xds, xdr, zds, zdr,
):
    loads = []
    for s in range(2):
        loads.append([
            pltpu.make_async_copy(ainv_in.at[0, s], ainv.at[s], in_sem.at[s, 0]),
            pltpu.make_async_copy(coup_in.at[s], coup.at[s], in_sem.at[s, 1]),
            pltpu.make_async_copy(src_in.at[0, s], src.at[s], in_sem.at[s, 2]),
        ])
        for load in loads[s]:
            load.start()
    dom, run = lax.axis_index("dom"), lax.axis_index("run")
    x, z = run // nz, run % nz
    y, odd = dom // 2, dom % 2 == 1
    even = jnp.logical_not(odd)
    ny = ndom // 2
    gate = jnp.where(odd, z == 0, z == nz - 1)
    last_x = x == nx - 1
    both = jnp.logical_and

    def at(d, xx, zz):
        return (d, xx * nz + zz)

    z_up, z_dn = at(dom, x, (z + 1) % nz), at(dom, x, (z + nz - 1) % nz)
    x_up, x_dn = at(dom, (x + 1) % nx, z), at(dom, (x + nx - 1) % nx, z)
    d_up, d_dn = at((dom + 2) % ndom, x, z), at((dom + ndom - 2) % ndom, x, z)
    twin = at(dom + 1 - 2 * (dom % 2), x, jnp.where(odd, z + nz - 1, z + 1) % nz)

    barrier = pltpu.get_barrier_semaphore()
    greet = (z_up, z_dn, x_up, x_dn, twin) + ((d_up, d_dn) if ny > 1 else ())
    for who in greet:
        pl.semaphore_signal(barrier, inc=1, device_id=who, device_id_type=MESH)

    for s in range(2):
        for load in loads[s]:
            load.wait()
        ar, ai = ainv[s, 0], ainv[s, 1]
        cr, ci = coup[s, 0], coup[s, 1]
        hr = (dot(ai, ci) - dot(ar, cr)).astype(BF16).astype(F32)
        hi = (-(dot(ar, ci) + dot(ai, cr))).astype(BF16).astype(F32)
        for t, (i, j) in enumerate(((0, 0), (0, H), (H, H))):
            top = jnp.concatenate(
                [hr[i : i + H, j : j + H].T, hi[i : i + H, j : j + H].T], axis=1
            )
            put_tile(wh.at[s], t, top.astype(BF16))
        sr_, si_ = src[s, 0], src[s, 1]
        pr_ = dot(ar, sr_) - dot(ai, si_)
        pi_ = dot(ar, si_) + dot(ai, sr_)
        for h in range(2):
            inj[s, :, 2 * h * H : (2 * h + 1) * H] = pr_[h * H : (h + 1) * H].T
            inj[s, :, (2 * h + 1) * H : (2 * h + 2) * H] = pi_[h * H : (h + 1) * H].T
    w1 = wh.at[1]
    tops = [wh[0, t * 2 * H : t * 2 * H + H, :] for t in range(3)]
    loc[A11_ROW:B_ROW, :] = stack(dot(tops[0], w1[tile(0), :]))
    loc[0:H, : 2 * H] = dot(jnp.concatenate([tops[1], tops[2]], axis=1), w1[tile(0, 2), :])
    loc[0:H, 2 * H :] = dot(tops[2], w1[tile(2), :])
    loc[B_ROW:, :] = full(inj[0], w1, mul2) + inj[1]
    put_weights(wm, loc)

    @pl.when(odd)
    def _():
        turn_a(loc, nloc, True)
        turn_b(loc, nloc)
        put_weights_n(wn, wb, nloc)

    pl.semaphore_wait(barrier, len(greet))

    def copy(src_ref, dst_ref, c, ssem, rsem, who, s_off=0):
        return pltpu.make_async_remote_copy(
            src_ref=src_ref.at[rows((c + s_off) * R, R)], dst_ref=dst_ref.at[rows(c * R, R)],
            send_sem=ssem, recv_sem=rsem, device_id=who, device_id_type=MESH,
        )

    def sent(buf, ssem):
        pltpu.make_async_remote_copy(
            src_ref=buf, dst_ref=buf, send_sem=ssem, recv_sem=zr.at[0],
            device_id=z_up, device_id_type=MESH,
        ).wait_send()

    def arrive(buf, rsem, c):
        copy(buf, buf, c, zs, rsem.at[c], z_up).wait_recv()

    def each(lo, hi, body):
        def step(c, carry):
            body(c)
            return carry

        lax.fori_loop(lo, hi, step, 0)

    def when(cond, body):
        pl.when(cond)(body)

    def chain_a(inp, outp, w, rsem, send):
        def a2(c):
            arrive(inp, rsem, c)
            outp[rows(c * R, R), :] = full(inp[rows(c * R, R), :], w, mul3)
            send(c)

        def a11(c):
            arrive(inp, rsem, c)
            outp[rows(c * R, R), :] = stack(mul3(unstack(inp[rows(c * R, R), :]), w, 0))
            send(c)

        each(0, NA2, a2)
        each(A11_CH, B_CH, a11)

    def chain_b(inp, outp, w, own, rsem, send):
        def bb(c):
            arrive(inp, rsem, c)
            r = rows(c * R, R)
            outp[r, :] = full(inp[r, :], w, mul3) + own[r, :]
            send(c)

        each(B_CH, NC, bb)

    def back_a(inp, outp, send):
        def top(c):
            arrive(inp, sr, c)
            v = inp[rows(c * R, R), :]
            outp[rows(c * R, R), :] = jnp.concatenate(
                [mul3(v[:, : 2 * H], wn, 0), mul3(v, wn, 1, 2)], axis=1
            )
            send(c)

        def low(c):
            arrive(inp, sr, c)
            outp[rows(c * R, R), :] = stack(mul3(unstack(inp[rows(c * R, R), :]), wn, 2))
            send(c)

        each(0, NA2, top)
        each(A11_CH, B_CH, low)

    def back_b(inp, outp, send):
        def bb(q):
            for half in range(2):
                k = q + half * (NB // 2)
                c = B_CH + k
                arrive(inp, sr, c)
                v = inp[rows(k * R, R), :]
                low = inp[rows(A11_ROW + q * R, R), half * 2 * H : (half + 1) * 2 * H]
                y1 = mul3(v, wb, 0, 2)
                y2 = mul3(low, wb, 1)
                r = rows(c * R, R)
                outp[r, :] = jnp.concatenate([y1, y2], axis=1) + inp[r, :]
                send(c)

        each(0, NB // 2, bb)

    def z_copy(c, src_ref):
        return copy(src_ref, ez, c, zs, zr.at[c], z_up)

    def s_copy(c, src_ref):
        return copy(src_ref, es, c, ss, sr.at[c], z_dn)

    def x_copy(c, src_ref):
        return copy(src_ref, ex, c, xs, xr.at[c], x_up)

    def p_copy(c):
        return copy(ox, ep, c, xs, pr.at[c], twin)

    def nothing(c):
        pass

    def t_copy(c):
        return copy(ox, sd, c, fs, xdr.at[c], twin, s_off=B_CH)

    def x_send(c):
        when(jnp.logical_not(last_x), lambda: x_copy(c, ox).start())
        when(both(last_x, both(odd, y < ny - 1)), lambda: p_copy(c).start())
        when(both(both(last_x, dom == 0), c >= B_CH), lambda: t_copy(c - B_CH).start())

    @pl.when(both(even, z == 0))
    def _():
        each(0, NC, lambda c: z_copy(c, loc).start())

    @pl.when(both(even, z > 0))
    def _():
        def send(c):
            when(jnp.logical_not(gate), lambda: z_copy(c, oz).start())
            when(both(gate, x == 0), lambda: x_copy(c, oz).start())

        chain_a(ez, oz, wm, zr, send)
        when(both(gate, x > 0), lambda: put_weights(wt, oz))
        when(both(gate, x == 1), lambda: chain_a(ex, ox, wt, xr, x_send))
        chain_b(ez, oz, wm, loc, zr, send)

    @pl.when(both(odd, z == nz - 1))
    def _():
        each(0, NC, lambda c: s_copy(c, nloc).start())

    @pl.when(both(odd, jnp.logical_and(z > 0, z < nz - 1)))
    def _():
        def send(c):
            s_copy(c, os).start()

        back_a(es, os, send)
        back_b(es, os, send)

    @pl.when(both(odd, z == 0))
    def _():
        def send(c):
            @pl.when(c == 0)
            def _():
                each(0, NC, lambda k: z_copy(k, loc).start())

        back_a(es, os, send)
        turn_a(os, oz, False)
        when(x == 0, lambda: each(0, B_CH, lambda c: x_copy(c, oz).start()))
        when(x > 0, lambda: put_weights(wt, oz))
        when(x == 1, lambda: chain_a(ex, ox, wt, xr, x_send))
        back_b(es, os, nothing)
        turn_b(os, oz)
        when(x == 0, lambda: each(B_CH, NC, lambda c: x_copy(c, oz).start()))

    @pl.when(both(gate, x > 0))
    def _():
        when(x > 1, lambda: chain_a(ex, ox, wt, xr, x_send))
        when(both(last_x, both(even, y > 0)), lambda: put_weights(wd, ox))
        chain_b(ex, ox, wt, oz, xr, x_send)
        put_weights(wex, ex)

    @pl.when(both(odd, z > 0))
    def _():
        @pl.when(z < nz - 1)
        def _():
            def send(c):
                z_copy(c, oz).start()

            chain_a(ez, oz, wm, zr, send)
            chain_b(ez, oz, wm, loc, zr, send)

        when(z == nz - 1, lambda: each(0, NC, lambda c: arrive(ez, zr, c)))

    when(z > 0, lambda: put_weights(we, ez))

    def spread(n, place, buf, ssem, rsem, up, dn):
        plus = (n - 1) // 2

        def up_copy(c):
            return copy(buf, buf, c, ssem.at[0], rsem.at[c], up)

        def dn_copy(c):
            return copy(buf, buf, c, ssem.at[1], rsem.at[c], dn)

        to_up = jnp.logical_or(place == n - 1, place < plus - 1) if plus else place < 0
        to_dn = place > plus

        def go(c):
            when(to_up, lambda: up_copy(c).start())
            when(to_dn, lambda: dn_copy(c).start())

        def drain():
            when(to_up, lambda: sent(buf, ssem.at[0]))
            when(to_dn, lambda: sent(buf, ssem.at[1]))

        return go, drain

    x_go, x_drain = spread(nx, x, sd, xds, xdr, x_up, x_dn)
    z_place = jnp.where(odd, z + nz - 1, z) % nz
    z_go, z_drain = spread(nz, z_place, sx, zds, zdr, z_up, z_dn)

    def first_copy(c):
        return copy(op, ed, c, ds, dr.at[c], d_up, s_off=B_CH)

    def d_copy(c):
        return copy(od, ed, c, ds, dr.at[c], d_up)

    def f_copy(c):
        return copy(o1, sd, c, fs, xdr.at[c], twin)

    head = both(gate, last_x)
    even_head = both(head, even)

    @pl.when(even_head)
    def _():
        if ny > 1:
            @pl.when(y < ny - 1)
            def _():
                each(0, B_CH, lambda c: arrive(ep, pr, c))
                put_weights(wep, ep)

                @pl.when(y > 0)
                def _():
                    for r in (0, H // 2):
                        op[r : r + H // 2, :] = full(ox[r : r + H // 2, :], wep, mul3)
                    op[A11_ROW:B_ROW, :] = stack(mul3(packed(ox), wep, 0))
                    put_weights(wp, op)

                def pair(c):
                    b = rows(B_ROW + c * R, R)
                    arrive(ep, pr, c + B_CH)
                    op[b, :] = full(ox[b, :], wep, mul3) + ep[b, :]
                    when(y == 0, lambda: first_copy(c).start())

                each(0, NB, pair)

            def step(c):
                r, b = rows(c * R, R), rows(B_ROW + c * R, R)
                arrive(ed, dr, c)

                @pl.when(y < ny - 1)
                def _():
                    od[r, :] = full(ed[r, :], wp, mul3) + op[b, :]
                    d_copy(c).start()

                sd[r, :] = ed[r, :]
                x_go(c)
                o1[r, :] = full(ed[r, :], wd, mul3) + ox[b, :]
                f_copy(c).start()

            when(y > 0, lambda: each(0, NB, step))

        @pl.when(y == 0)
        def _():
            sd[...] = jnp.zeros_like(sd)
            each(0, NB, x_go)

    @pl.when(gate)
    def _():
        def step(c):
            r = rows(c * R, R)

            @pl.when(jnp.logical_not(even_head))
            def _():
                arrive(sd, xdr, c)
                x_go(c)

            @pl.when(x == 0)
            def _():
                sx[r, :] = sd[r, :]

            @pl.when(x > 0)
            def _():
                sx[r, :] = full(sd[r, :], wex, mul3) + ex[rows(B_ROW + c * R, R), :]

            z_go(c)

        each(0, NB, step)

    def finish(start, size):
        r = rows(start, size)

        @pl.when(z == 0)
        def _():
            fin[0, r, :] = sx[r, :]

        @pl.when(z > 0)
        def _():
            fin[0, r, :] = full(sx[r, :], we, mul3) + ez[rows(B_ROW + start, size), :]

        s0 = full(fin[0, r, :], wh.at[0], mul2) + inj[0, r, :]
        fin[0, r, :] = s0
        fin[1, r, :] = full(s0, wh.at[1], mul2) + inj[1, r, :]

    @pl.when(jnp.logical_not(gate))
    def _():
        def pass_on(c):
            arrive(sx, zdr, c)
            z_go(c)

        each(0, NB, pass_on)

    each(0, 2, lambda c: finish(c * (H // 2), H // 2))

    for s in range(2):
        for p in range(2):
            for h in range(2):
                k = (2 * h + p) * H
                out[0, s, p, h * H : (h + 1) * H, :] = fin[s, :, k : k + H].T

    when(jnp.logical_or(z == 0, z < nz - 1), lambda: sent(ez, zs))
    when(both(odd, z > 0), lambda: sent(es, ss))
    when(both(gate, jnp.logical_or(jnp.logical_not(last_x), both(odd, y < ny - 1))), lambda: sent(ex, xs))
    when(even_head, lambda: sent(sd, fs))
    if ny > 1:
        when(both(even_head, y < ny - 1), lambda: sent(ed, ds))
    when(gate, x_drain)
    z_drain()


def build(mesh, nx):
    ndom, nrun = mesh.shape["dom"], mesh.shape["run"]
    nz = nrun // nx

    def shards(ainv, coupling, source):
        big = pltpu.VMEM((ROWS, 4 * H), F32)
        half = pltpu.VMEM((H, 4 * H), F32)
        weights = pltpu.VMEM((2, 6 * H, 2 * H), BF16)
        sem = pltpu.SemaphoreType.DMA

        def body(*refs):
            kernel(ndom, nx, nz, *refs)

        vm = pl.BlockSpec(memory_space=pltpu.VMEM)
        return pl.pallas_call(
            body,
            out_shape=jax.ShapeDtypeStruct(source.shape, F32),
            in_specs=[pl.BlockSpec(memory_space=pltpu.HBM)] * 3,
            out_specs=vm,
            scratch_shapes=[
                pltpu.VMEM((2, 2, 2 * H, 2 * H), BF16),
                pltpu.VMEM((2, 2, 2 * H, 2 * H), BF16),
                pltpu.VMEM((2, 2, 2 * H, H), BF16),
                sem((2, 3)),
                big, big, big, big, big, big, big, big, big, big,
                half, half, half, half, half,
                weights, weights, weights, weights, weights, weights, weights, weights,
                pltpu.VMEM((2, 4 * H, 2 * H), BF16),
                pltpu.VMEM((2, 6 * H, 2 * H), BF16),
                pltpu.VMEM((2, H, 4 * H), F32),
                pltpu.VMEM((2, H, 4 * H), F32),
                sem, sem((NC,)), sem, sem((NC,)), sem, sem((NC,)), sem((NC,)),
                sem, sem((NB,)), sem,
                sem((2,)), sem((NB,)), sem((2,)), sem((NB,)),
            ],
            compiler_params=pltpu.CompilerParams(
                collective_id=0, has_side_effects=True, vmem_limit_bytes=48 * 1024 * 1024
            ),
            name="sweep",
        )(*(pltpu.with_memory_space_constraint(a, pltpu.HBM) for a in (ainv, coupling, source)))

    in_specs = (
        P(None, ("dom", "run"), None, None, None),
        P(("dom", "run"), None, None, None),
        P(None, ("dom", "run"), None, None, None),
    )
    out_specs = P(None, ("dom", "run"), None, None, None)
    return jax.shard_map(shards, mesh=mesh, in_specs=in_specs, out_specs=out_specs, check_vma=False)


def solution(mesh):
    return build(mesh, NX)
```

```python
import jax
import jax.numpy as jnp
from jax import lax
from jax.experimental import pallas as pl
from jax.experimental.pallas import tpu as pltpu
from jax.sharding import PartitionSpec as P

MESH = pl.DeviceIdType.MESH
F32 = jnp.float32
BF16 = jnp.bfloat16

NX = 4
H = 128
R = 16
NA2 = H // R
NA11 = H // 2 // R
NB = H // R
A11_ROW = H
B_ROW = H + H // 2
ROWS = B_ROW + H
A11_CH = NA2
B_CH = NA2 + NA11
NC = B_CH + NB


def dot(a, b):
    return lax.dot_general(a, b, (((1,), (0,)), ((), ())), preferred_element_type=F32)


def split(x):
    hi = x.astype(BF16)
    return hi, (x - hi.astype(F32)).astype(BF16)


def rows(start, size):
    return pl.ds(pl.multiple_of(start, 8), size)


def put_tile(w, t, top):
    k = t * 2 * H
    w[k : k + H, :] = top
    w[k + H : k + 2 * H, 0:H] = -top[:, H:]
    w[k + H : k + 2 * H, H:] = top[:, :H]


def tile(t, n=1):
    return slice(t * 2 * H, (t + n) * 2 * H)


def put_pair(w, t, top):
    hi, lo = split(top)
    put_tile(w.at[0], t, hi)
    put_tile(w.at[1], t, lo)


def unstack(v):
    return jnp.concatenate([v[:, : 2 * H], v[:, 2 * H :]], axis=0)


def stack(y):
    n = y.shape[0] // 2
    return jnp.concatenate([y[:n], y[n:]], axis=1)


def packed(buf):
    return unstack(buf[A11_ROW:B_ROW, :])


def put_weights(w, buf):
    put_pair(w, 0, packed(buf))
    put_pair(w, 1, buf[0:H, 0 : 2 * H])
    put_pair(w, 2, buf[0:H, 2 * H :])


def put_weights_n(w, wb, buf):
    put_pair(w, 0, buf[0:H, 0 : 2 * H])
    put_pair(w, 1, buf[0:H, 2 * H :])
    put_pair(w, 2, packed(buf))
    put_pair(wb, 0, buf[B_ROW:, 0 : 2 * H])
    put_pair(wb, 1, buf[B_ROW:, 2 * H :])


def flip(v):
    return jnp.concatenate([v[:, k : k + H].T for k in range(0, v.shape[1], H)], axis=1)


def turn_a(src, dst):
    dst[0:H, 0 : 2 * H] = flip(packed(src))
    dst[0:H, 2 * H :] = flip(src[0:H, 0 : 2 * H])
    dst[A11_ROW:B_ROW, :] = stack(flip(src[0:H, 2 * H :]))


def turn_b(src, dst):
    dst[B_ROW:, :] = flip(src[B_ROW:, :])


def mul3(x, w, t, k=1):
    n = x.shape[0]
    hi, lo = split(x)
    both = dot(jnp.concatenate([hi, lo], axis=0), w[0, tile(t, k), :])
    return both[:n] + both[n:] + dot(hi, w[1, tile(t, k), :])


def mul2(x, w, t, k=1):
    n = x.shape[0]
    hi, lo = split(x)
    both = dot(jnp.concatenate([hi, lo], axis=0), w[tile(t, k), :])
    return both[:n] + both[n:]


def full(x, w, mul):
    return jnp.concatenate([mul(x, w, 0, 2), mul(x[:, 2 * H :], w, 2)], axis=1)


def kernel(
    ndom, nx, nz, ainv_in, coup_in, src_in, out,
    ainv, coup, src, in_sem,
    loc, ez, oz, ex, ox, es, os, nloc, ep, op, ed, od, o1, sd, sx,
    wm, we, wt, wex, wd, wn, wp, wep, wb, wh, inj, fin,
    zs, zr, xs, xr, ss, sr, pr, ds, dr, fs, xds, xdr, zds, zdr,
):
    loads = []
    for s in range(2):
        loads.append([
            pltpu.make_async_copy(ainv_in.at[0, s], ainv.at[s], in_sem.at[s, 0]),
            pltpu.make_async_copy(coup_in.at[s], coup.at[s], in_sem.at[s, 1]),
            pltpu.make_async_copy(src_in.at[0, s], src.at[s], in_sem.at[s, 2]),
        ])
        for load in loads[s]:
            load.start()
    dom, run = lax.axis_index("dom"), lax.axis_index("run")
    x, z = run // nz, run % nz
    y, odd = dom // 2, dom % 2 == 1
    even = jnp.logical_not(odd)
    ny = ndom // 2
    gate = jnp.where(odd, z == 0, z == nz - 1)
    last_x = x == nx - 1
    both = jnp.logical_and

    def at(d, xx, zz):
        return (d, xx * nz + zz)

    z_up, z_dn = at(dom, x, (z + 1) % nz), at(dom, x, (z + nz - 1) % nz)
    x_up, x_dn = at(dom, (x + 1) % nx, z), at(dom, (x + nx - 1) % nx, z)
    d_up, d_dn = at((dom + 2) % ndom, x, z), at((dom + ndom - 2) % ndom, x, z)
    twin = at(dom + 1 - 2 * (dom % 2), x, jnp.where(odd, z + nz - 1, z + 1) % nz)

    barrier = pltpu.get_barrier_semaphore()
    greet = (z_up, z_dn, x_up, x_dn, twin) + ((d_up, d_dn) if ny > 1 else ())
    for who in greet:
        pl.semaphore_signal(barrier, inc=1, device_id=who, device_id_type=MESH)

    for s in range(2):
        for load in loads[s]:
            load.wait()
        ar, ai = ainv[s, 0], ainv[s, 1]
        cr, ci = coup[s, 0], coup[s, 1]
        hr = (dot(ai, ci) - dot(ar, cr)).astype(BF16).astype(F32)
        hi = (-(dot(ar, ci) + dot(ai, cr))).astype(BF16).astype(F32)
        for t, (i, j) in enumerate(((0, 0), (0, H), (H, H))):
            top = jnp.concatenate(
                [hr[i : i + H, j : j + H].T, hi[i : i + H, j : j + H].T], axis=1
            )
            put_tile(wh.at[s], t, top.astype(BF16))
        sr_, si_ = src[s, 0], src[s, 1]
        pr_ = dot(ar, sr_) - dot(ai, si_)
        pi_ = dot(ar, si_) + dot(ai, sr_)
        for h in range(2):
            inj[s, :, 2 * h * H : (2 * h + 1) * H] = pr_[h * H : (h + 1) * H].T
            inj[s, :, (2 * h + 1) * H : (2 * h + 2) * H] = pi_[h * H : (h + 1) * H].T
    w1 = wh.at[1]
    tops = [wh[0, t * 2 * H : t * 2 * H + H, :] for t in range(3)]
    loc[A11_ROW:B_ROW, :] = stack(dot(tops[0], w1[tile(0), :]))
    loc[0:H, : 2 * H] = dot(jnp.concatenate([tops[1], tops[2]], axis=1), w1[tile(0, 2), :])
    loc[0:H, 2 * H :] = dot(tops[2], w1[tile(2), :])
    loc[B_ROW:, :] = full(inj[0], w1, mul2) + inj[1]
    put_weights(wm, loc)

    @pl.when(odd)
    def _():
        turn_a(loc, nloc)
        turn_b(loc, nloc)
        put_weights_n(wn, wb, nloc)

    pl.semaphore_wait(barrier, len(greet))

    def copy(src_ref, dst_ref, c, ssem, rsem, who, s_off=0):
        return pltpu.make_async_remote_copy(
            src_ref=src_ref.at[rows((c + s_off) * R, R)], dst_ref=dst_ref.at[rows(c * R, R)],
            send_sem=ssem, recv_sem=rsem, device_id=who, device_id_type=MESH,
        )

    def sent(buf, ssem):
        pltpu.make_async_remote_copy(
            src_ref=buf, dst_ref=buf, send_sem=ssem, recv_sem=zr.at[0],
            device_id=z_up, device_id_type=MESH,
        ).wait_send()

    def arrive(buf, rsem, c):
        copy(buf, buf, c, zs, rsem.at[c], z_up).wait_recv()

    def each(lo, hi, body):
        def step(c, carry):
            body(c)
            return carry

        lax.fori_loop(lo, hi, step, 0)

    def when(cond, body):
        pl.when(cond)(body)

    def chain_a(inp, outp, w, rsem, send):
        def a2(c):
            arrive(inp, rsem, c)
            outp[rows(c * R, R), :] = full(inp[rows(c * R, R), :], w, mul3)
            send(c)

        def a11(c):
            arrive(inp, rsem, c)
            outp[rows(c * R, R), :] = stack(mul3(unstack(inp[rows(c * R, R), :]), w, 0))
            send(c)

        each(A11_CH, B_CH, a11)
        each(0, NA2, a2)

    def chain_b(inp, outp, w, own, rsem, send):
        def bb(c):
            arrive(inp, rsem, c)
            r = rows(c * R, R)
            outp[r, :] = full(inp[r, :], w, mul3) + own[r, :]
            send(c)

        each(B_CH, NC, bb)

    def back_top(inp, outp, send):
        def top(c):
            arrive(inp, sr, c)
            v = inp[rows(c * R, R), :]
            outp[rows(c * R, R), :] = jnp.concatenate(
                [mul3(v[:, : 2 * H], wn, 0), mul3(v, wn, 1, 2)], axis=1
            )
            send(c)

        each(0, NA2, top)

    def back_low(inp, outp, send):
        def low(c):
            arrive(inp, sr, c)
            outp[rows(c * R, R), :] = stack(mul3(unstack(inp[rows(c * R, R), :]), wn, 2))
            send(c)

        each(A11_CH, B_CH, low)

    def back_b(inp, outp, send):
        def bb(q):
            for half in range(2):
                k = q + half * (NB // 2)
                c = B_CH + k
                arrive(inp, sr, c)
                v = inp[rows(k * R, R), :]
                low = inp[rows(A11_ROW + q * R, R), half * 2 * H : (half + 1) * 2 * H]
                y1 = mul3(v, wb, 0, 2)
                y2 = mul3(low, wb, 1)
                r = rows(c * R, R)
                outp[r, :] = jnp.concatenate([y1, y2], axis=1) + inp[r, :]
                send(c)

        each(0, NB // 2, bb)

    def z_copy(c, src_ref):
        return copy(src_ref, ez, c, zs, zr.at[c], z_up)

    def s_copy(c, src_ref):
        return copy(src_ref, es, c, ss, sr.at[c], z_dn)

    def x_copy(c, src_ref):
        return copy(src_ref, ex, c, xs, xr.at[c], x_up)

    def p_copy(c):
        return copy(ox, ep, c, xs, pr.at[c], twin)

    def nothing(c):
        pass

    def t_copy(c):
        return copy(ox, sd, c, fs, xdr.at[c], twin, s_off=B_CH)

    def x_send(c):
        when(jnp.logical_not(last_x), lambda: x_copy(c, ox).start())
        when(both(last_x, both(odd, y < ny - 1)), lambda: p_copy(c).start())
        when(both(both(last_x, dom == 0), c >= B_CH), lambda: t_copy(c - B_CH).start())

    @pl.when(both(even, z == 0))
    def _():
        each(0, NC, lambda c: z_copy(c, loc).start())

    @pl.when(both(even, z > 0))
    def _():
        def send(c):
            when(jnp.logical_not(gate), lambda: z_copy(c, oz).start())
            when(both(gate, x == 0), lambda: x_copy(c, oz).start())

        chain_a(ez, oz, wm, zr, send)
        when(both(gate, x > 0), lambda: put_weights(wt, oz))
        when(both(gate, x == 1), lambda: chain_a(ex, ox, wt, xr, x_send))
        chain_b(ez, oz, wm, loc, zr, send)

    @pl.when(both(odd, z == nz - 1))
    def _():
        each(0, NC, lambda c: s_copy(c, nloc).start())

    @pl.when(both(odd, jnp.logical_and(z > 0, z < nz - 1)))
    def _():
        def send(c):
            s_copy(c, os).start()

        back_top(es, os, send)
        back_low(es, os, send)
        back_b(es, os, send)

    @pl.when(both(odd, z == 0))
    def _():
        def send(c):
            @pl.when(c == 0)
            def _():
                each(0, NC, lambda k: z_copy(k, loc).start())

        back_top(es, os, send)
        oz[A11_ROW:B_ROW, :] = stack(flip(os[0:H, 0 : 2 * H]))
        when(x == 0, lambda: each(A11_CH, B_CH, lambda c: x_copy(c, oz).start()))
        back_low(es, os, send)
        oz[0:H, 0 : 2 * H] = flip(os[0:H, 2 * H :])
        oz[0:H, 2 * H :] = flip(packed(os))
        when(x == 0, lambda: each(0, NA2, lambda c: x_copy(c, oz).start()))
        when(x > 0, lambda: put_weights(wt, oz))
        when(x == 1, lambda: chain_a(ex, ox, wt, xr, x_send))
        back_b(es, os, nothing)
        turn_b(os, oz)
        when(x == 0, lambda: each(B_CH, NC, lambda c: x_copy(c, oz).start()))

    @pl.when(both(gate, x > 0))
    def _():
        when(x > 1, lambda: chain_a(ex, ox, wt, xr, x_send))
        when(both(last_x, both(even, y > 0)), lambda: put_weights(wd, ox))
        chain_b(ex, ox, wt, oz, xr, x_send)
        put_weights(wex, ex)

    @pl.when(both(odd, z > 0))
    def _():
        @pl.when(z < nz - 1)
        def _():
            def send(c):
                z_copy(c, oz).start()

            chain_a(ez, oz, wm, zr, send)
            chain_b(ez, oz, wm, loc, zr, send)

        when(z == nz - 1, lambda: each(0, NC, lambda c: arrive(ez, zr, c)))

    when(z > 0, lambda: put_weights(we, ez))

    def spread(n, place, plus, buf, ssem, rsem, up, dn):
        def up_copy(c):
            return copy(buf, buf, c, ssem.at[0], rsem.at[c], up)

        def dn_copy(c):
            return copy(buf, buf, c, ssem.at[1], rsem.at[c], dn)

        to_up = jnp.logical_or(both(place == n - 1, plus > 0), place < plus - 1)
        to_dn = both(place > plus, plus < n - 1)

        def go(c):
            when(to_up, lambda: up_copy(c).start())
            when(to_dn, lambda: dn_copy(c).start())

        def drain():
            when(to_up, lambda: sent(buf, ssem.at[0]))
            when(to_dn, lambda: sent(buf, ssem.at[1]))

        return go, drain

    x_go, x_drain = spread(nx, x, (nx - 1) // 2, sd, xds, xdr, x_up, x_dn)
    z_place = jnp.where(odd, z + nz - 1, z) % nz
    z_go, z_drain = spread(nz, z_place, jnp.where(odd, nz // 2, (nz - 1) // 2), sx, zds, zdr, z_up, z_dn)

    def first_copy(c):
        return copy(op, ed, c, ds, dr.at[c], d_up, s_off=B_CH)

    def d_copy(c):
        return copy(od, ed, c, ds, dr.at[c], d_up)

    def f_copy(c):
        return copy(o1, sd, c, fs, xdr.at[c], twin)

    head = both(gate, last_x)
    even_head = both(head, even)

    @pl.when(even_head)
    def _():
        if ny > 1:
            @pl.when(y < ny - 1)
            def _():
                each(0, B_CH, lambda c: arrive(ep, pr, c))
                put_weights(wep, ep)

                @pl.when(y > 0)
                def _():
                    for r in (0, H // 2):
                        op[r : r + H // 2, :] = full(ox[r : r + H // 2, :], wep, mul3)
                    op[A11_ROW:B_ROW, :] = stack(mul3(packed(ox), wep, 0))
                    put_weights(wp, op)

                def pair(c):
                    b = rows(B_ROW + c * R, R)
                    arrive(ep, pr, c + B_CH)
                    op[b, :] = full(ox[b, :], wep, mul3) + ep[b, :]
                    when(y == 0, lambda: first_copy(c).start())

                each(0, NB, pair)

            def step(q):
                for half in range(2):
                    c = 2 * q + half
                    r, b = rows(c * R, R), rows(B_ROW + c * R, R)
                    arrive(ed, dr, c)

                    @pl.when(y < ny - 1)
                    def _():
                        od[r, :] = full(ed[r, :], wp, mul3) + op[b, :]
                        d_copy(c).start()

                    sd[r, :] = ed[r, :]
                    x_go(c)
                r, b = rows(2 * q * R, 2 * R), rows(B_ROW + 2 * q * R, 2 * R)
                o1[r, :] = full(ed[r, :], wd, mul3) + ox[b, :]
                for half in range(2):
                    f_copy(2 * q + half).start()

            when(y > 0, lambda: each(0, NB // 2, step))

        @pl.when(y == 0)
        def _():
            sd[...] = jnp.zeros_like(sd)
            each(0, NB, x_go)

    @pl.when(gate)
    def _():
        def step(c):
            r = rows(c * R, R)

            @pl.when(jnp.logical_not(even_head))
            def _():
                arrive(sd, xdr, c)
                x_go(c)

            @pl.when(x == 0)
            def _():
                sx[r, :] = sd[r, :]

            @pl.when(x > 0)
            def _():
                sx[r, :] = full(sd[r, :], wex, mul3) + ex[rows(B_ROW + c * R, R), :]

            z_go(c)

        each(0, NB, step)

    def finish(start, size):
        r = rows(start, size)

        @pl.when(z == 0)
        def _():
            fin[0, r, :] = sx[r, :]

        @pl.when(z > 0)
        def _():
            fin[0, r, :] = full(sx[r, :], we, mul3) + ez[rows(B_ROW + start, size), :]

        s0 = full(fin[0, r, :], wh.at[0], mul2) + inj[0, r, :]
        fin[0, r, :] = s0
        fin[1, r, :] = full(s0, wh.at[1], mul2) + inj[1, r, :]

    @pl.when(jnp.logical_not(gate))
    def _():
        def pass_on(c):
            arrive(sx, zdr, c)
            z_go(c)

        for half in range(2):
            each(half * (NB // 2), (half + 1) * (NB // 2), pass_on)
            finish(half * (H // 2), H // 2)

    when(gate, lambda: each(0, 2, lambda c: finish(c * (H // 2), H // 2)))

    for s in range(2):
        for p in range(2):
            for h in range(2):
                k = (2 * h + p) * H
                out[0, s, p, h * H : (h + 1) * H, :] = fin[s, :, k : k + H].T

    when(jnp.logical_or(z == 0, z < nz - 1), lambda: sent(ez, zs))
    when(both(odd, z > 0), lambda: sent(es, ss))
    when(both(gate, jnp.logical_or(jnp.logical_not(last_x), both(odd, y < ny - 1))), lambda: sent(ex, xs))
    when(even_head, lambda: sent(sd, fs))
    if ny > 1:
        when(both(even_head, y < ny - 1), lambda: sent(ed, ds))
    when(gate, x_drain)
    z_drain()


def build(mesh, nx):
    ndom, nrun = mesh.shape["dom"], mesh.shape["run"]
    nz = nrun // nx

    def shards(ainv, coupling, source):
        big = pltpu.VMEM((ROWS, 4 * H), F32)
        half = pltpu.VMEM((H, 4 * H), F32)
        weights = pltpu.VMEM((2, 6 * H, 2 * H), BF16)
        sem = pltpu.SemaphoreType.DMA

        def body(*refs):
            kernel(ndom, nx, nz, *refs)

        vm = pl.BlockSpec(memory_space=pltpu.VMEM)
        return pl.pallas_call(
            body,
            out_shape=jax.ShapeDtypeStruct(source.shape, F32),
            in_specs=[pl.BlockSpec(memory_space=pltpu.HBM)] * 3,
            out_specs=vm,
            scratch_shapes=[
                pltpu.VMEM((2, 2, 2 * H, 2 * H), BF16),
                pltpu.VMEM((2, 2, 2 * H, 2 * H), BF16),
                pltpu.VMEM((2, 2, 2 * H, H), BF16),
                sem((2, 3)),
                big, big, big, big, big, big, big, big, big, big,
                half, half, half, half, half,
                weights, weights, weights, weights, weights, weights, weights, weights,
                pltpu.VMEM((2, 4 * H, 2 * H), BF16),
                pltpu.VMEM((2, 6 * H, 2 * H), BF16),
                pltpu.VMEM((2, H, 4 * H), F32),
                pltpu.VMEM((2, H, 4 * H), F32),
                sem, sem((NC,)), sem, sem((NC,)), sem, sem((NC,)), sem((NC,)),
                sem, sem((NB,)), sem,
                sem((2,)), sem((NB,)), sem((2,)), sem((NB,)),
            ],
            compiler_params=pltpu.CompilerParams(
                collective_id=0, has_side_effects=True, vmem_limit_bytes=48 * 1024 * 1024
            ),
            name="sweep",
        )(*(pltpu.with_memory_space_constraint(a, pltpu.HBM) for a in (ainv, coupling, source)))

    in_specs = (
        P(None, ("dom", "run"), None, None, None),
        P(("dom", "run"), None, None, None),
        P(None, ("dom", "run"), None, None, None),
    )
    out_specs = P(None, ("dom", "run"), None, None, None)
    return jax.shard_map(shards, mesh=mesh, in_specs=in_specs, out_specs=out_specs, check_vma=False)


def solution(mesh):
    return build(mesh, NX)
```

```python
import jax
import jax.numpy as jnp
from jax import lax
from jax.experimental import pallas as pl
from jax.experimental.pallas import tpu as pltpu
from jax.sharding import PartitionSpec as P

MESH = pl.DeviceIdType.MESH
F32 = jnp.float32
BF16 = jnp.bfloat16

NX = 4
H = 128
R = 16
NA2 = H // R
NA11 = H // 2 // R
NB = H // R
A11_ROW = H
B_ROW = H + H // 2
ROWS = B_ROW + H
A11_CH = NA2
B_CH = NA2 + NA11
NC = B_CH + NB


def dot(a, b):
    return lax.dot_general(a, b, (((1,), (0,)), ((), ())), preferred_element_type=F32)


def split(x):
    hi = x.astype(BF16)
    return hi, (x - hi.astype(F32)).astype(BF16)


def rows(start, size):
    return pl.ds(pl.multiple_of(start, 8), size)


def put_tile(w, t, top):
    k = t * 2 * H
    w[k : k + H, :] = top
    w[k + H : k + 2 * H, 0:H] = -top[:, H:]
    w[k + H : k + 2 * H, H:] = top[:, :H]


def tile(t, n=1):
    return slice(t * 2 * H, (t + n) * 2 * H)


def put_pair(w, t, top):
    hi, lo = split(top)
    put_tile(w.at[0], t, hi)
    put_tile(w.at[1], t, lo)


def unstack(v):
    return jnp.concatenate([v[:, : 2 * H], v[:, 2 * H :]], axis=0)


def stack(y):
    n = y.shape[0] // 2
    return jnp.concatenate([y[:n], y[n:]], axis=1)


def packed(buf):
    return unstack(buf[A11_ROW:B_ROW, :])


def put_weights(w, buf):
    put_pair(w, 0, packed(buf))
    put_pair(w, 1, buf[0:H, 0 : 2 * H])
    put_pair(w, 2, buf[0:H, 2 * H :])


def put_weights_n(w, wb, buf):
    put_pair(w, 0, buf[0:H, 0 : 2 * H])
    put_pair(w, 1, buf[0:H, 2 * H :])
    put_pair(w, 2, packed(buf))
    put_pair(wb, 0, buf[B_ROW:, 0 : 2 * H])
    put_pair(wb, 1, buf[B_ROW:, 2 * H :])


def flip(v):
    return jnp.concatenate([v[:, k : k + H].T for k in range(0, v.shape[1], H)], axis=1)


def turn_a(src, dst):
    dst[0:H, 0 : 2 * H] = flip(packed(src))
    dst[0:H, 2 * H :] = flip(src[0:H, 0 : 2 * H])
    dst[A11_ROW:B_ROW, :] = stack(flip(src[0:H, 2 * H :]))


def turn_b(src, dst):
    dst[B_ROW:, :] = flip(src[B_ROW:, :])


def mul3(x, w, t, k=1):
    n = x.shape[0]
    hi, lo = split(x)
    both = dot(jnp.concatenate([hi, lo], axis=0), w[0, tile(t, k), :])
    return both[:n] + both[n:] + dot(hi, w[1, tile(t, k), :])


def mul2(x, w, t, k=1):
    n = x.shape[0]
    hi, lo = split(x)
    both = dot(jnp.concatenate([hi, lo], axis=0), w[tile(t, k), :])
    return both[:n] + both[n:]


def full(x, w, mul):
    return jnp.concatenate([mul(x, w, 0, 2), mul(x[:, 2 * H :], w, 2)], axis=1)


def kernel(
    ndom, nx, nz, ainv_in, coup_in, src_in, out,
    ainv, coup, src, in_sem,
    loc, ez, oz, ex, ox, es, os, nloc, ep, op, ed, od, o1, sd, sx,
    wm, we, wt, wex, wd, wn, wp, wep, wb, wh, inj, fin,
    zs, zr, xs, xr, ss, sr, pr, ds, dr, fs, xds, xdr, zds, zdr,
):
    loads = []
    for s in range(2):
        loads.append([
            pltpu.make_async_copy(ainv_in.at[0, s], ainv.at[s], in_sem.at[s, 0]),
            pltpu.make_async_copy(coup_in.at[s], coup.at[s], in_sem.at[s, 1]),
            pltpu.make_async_copy(src_in.at[0, s], src.at[s], in_sem.at[s, 2]),
        ])
        for load in loads[s]:
            load.start()
    dom, run = lax.axis_index("dom"), lax.axis_index("run")
    x, z = run // nz, run % nz
    y, odd = dom // 2, dom % 2 == 1
    even = jnp.logical_not(odd)
    ny = ndom // 2
    gate = jnp.where(odd, z == 0, z == nz - 1)
    last_x = x == nx - 1
    both = jnp.logical_and

    def at(d, xx, zz):
        return (d, xx * nz + zz)

    z_up, z_dn = at(dom, x, (z + 1) % nz), at(dom, x, (z + nz - 1) % nz)
    x_up, x_dn = at(dom, (x + 1) % nx, z), at(dom, (x + nx - 1) % nx, z)
    d_up, d_dn = at((dom + 2) % ndom, x, z), at((dom + ndom - 2) % ndom, x, z)
    twin = at(dom + 1 - 2 * (dom % 2), x, jnp.where(odd, z + nz - 1, z + 1) % nz)

    barrier = pltpu.get_barrier_semaphore()
    greet = (z_up, z_dn, x_up, x_dn, twin) + ((d_up, d_dn) if ny > 1 else ())
    for who in greet:
        pl.semaphore_signal(barrier, inc=1, device_id=who, device_id_type=MESH)

    for s in range(2):
        for load in loads[s]:
            load.wait()
        ar, ai = ainv[s, 0], ainv[s, 1]
        cr, ci = coup[s, 0], coup[s, 1]
        hr = (dot(ai, ci) - dot(ar, cr)).astype(BF16).astype(F32)
        hi = (-(dot(ar, ci) + dot(ai, cr))).astype(BF16).astype(F32)
        for t, (i, j) in enumerate(((0, 0), (0, H), (H, H))):
            top = jnp.concatenate(
                [hr[i : i + H, j : j + H].T, hi[i : i + H, j : j + H].T], axis=1
            )
            put_tile(wh.at[s], t, top.astype(BF16))
        sr_, si_ = src[s, 0], src[s, 1]
        pr_ = dot(ar, sr_) - dot(ai, si_)
        pi_ = dot(ar, si_) + dot(ai, sr_)
        for h in range(2):
            inj[s, :, 2 * h * H : (2 * h + 1) * H] = pr_[h * H : (h + 1) * H].T
            inj[s, :, (2 * h + 1) * H : (2 * h + 2) * H] = pi_[h * H : (h + 1) * H].T
    w1 = wh.at[1]
    tops = [wh[0, t * 2 * H : t * 2 * H + H, :] for t in range(3)]
    loc[A11_ROW:B_ROW, :] = stack(dot(tops[0], w1[tile(0), :]))
    loc[0:H, : 2 * H] = dot(jnp.concatenate([tops[1], tops[2]], axis=1), w1[tile(0, 2), :])
    loc[0:H, 2 * H :] = dot(tops[2], w1[tile(2), :])
    loc[B_ROW:, :] = full(inj[0], w1, mul2) + inj[1]
    put_weights(wm, loc)

    @pl.when(odd)
    def _():
        turn_a(loc, nloc)
        turn_b(loc, nloc)
        put_weights_n(wn, wb, nloc)

    pl.semaphore_wait(barrier, len(greet))

    def copy(src_ref, dst_ref, c, ssem, rsem, who, s_off=0):
        return pltpu.make_async_remote_copy(
            src_ref=src_ref.at[rows((c + s_off) * R, R)], dst_ref=dst_ref.at[rows(c * R, R)],
            send_sem=ssem, recv_sem=rsem, device_id=who, device_id_type=MESH,
        )

    def sent(buf, ssem):
        pltpu.make_async_remote_copy(
            src_ref=buf, dst_ref=buf, send_sem=ssem, recv_sem=zr.at[0],
            device_id=z_up, device_id_type=MESH,
        ).wait_send()

    def arrive(buf, rsem, c):
        copy(buf, buf, c, zs, rsem.at[c], z_up).wait_recv()

    def each(lo, hi, body):
        def step(c, carry):
            body(c)
            return carry

        lax.fori_loop(lo, hi, step, 0)

    def when(cond, body):
        pl.when(cond)(body)

    def chain_a(inp, outp, w, rsem, send):
        def a2(c):
            arrive(inp, rsem, c)
            outp[rows(c * R, R), :] = full(inp[rows(c * R, R), :], w, mul3)
            send(c)

        def a11(c):
            arrive(inp, rsem, c)
            outp[rows(c * R, R), :] = stack(mul3(unstack(inp[rows(c * R, R), :]), w, 0))
            send(c)

        each(A11_CH, B_CH, a11)
        each(0, NA2, a2)

    def chain_b(inp, outp, w, own, rsem, send):
        def bb(c):
            arrive(inp, rsem, c)
            r = rows(c * R, R)
            outp[r, :] = full(inp[r, :], w, mul3) + own[r, :]
            send(c)

        each(B_CH, NC, bb)

    def back_top(inp, outp, send):
        def top(c):
            arrive(inp, sr, c)
            v = inp[rows(c * R, R), :]
            outp[rows(c * R, R), :] = jnp.concatenate(
                [mul3(v[:, : 2 * H], wn, 0), mul3(v, wn, 1, 2)], axis=1
            )
            send(c)

        each(0, NA2, top)

    def back_low(inp, outp, send):
        def low(c):
            arrive(inp, sr, c)
            outp[rows(c * R, R), :] = stack(mul3(unstack(inp[rows(c * R, R), :]), wn, 2))
            send(c)

        each(A11_CH, B_CH, low)

    def back_b(inp, outp, send):
        def bb(q):
            for half in range(2):
                k = q + half * (NB // 2)
                c = B_CH + k
                arrive(inp, sr, c)
                v = inp[rows(k * R, R), :]
                low = inp[rows(A11_ROW + q * R, R), half * 2 * H : (half + 1) * 2 * H]
                y1 = mul3(v, wb, 0, 2)
                y2 = mul3(low, wb, 1)
                r = rows(c * R, R)
                outp[r, :] = jnp.concatenate([y1, y2], axis=1) + inp[r, :]
                send(c)

        each(0, NB // 2, bb)

    def z_copy(c, src_ref):
        return copy(src_ref, ez, c, zs, zr.at[c], z_up)

    def s_copy(c, src_ref):
        return copy(src_ref, es, c, ss, sr.at[c], z_dn)

    def x_copy(c, src_ref):
        return copy(src_ref, ex, c, xs, xr.at[c], x_up)

    def p_copy(c):
        return copy(ox, ep, c, xs, pr.at[c], twin)

    def nothing(c):
        pass

    def t_copy(c):
        return copy(ox, sd, c, fs, xdr.at[c], twin, s_off=B_CH)

    def x_send(c):
        when(jnp.logical_not(last_x), lambda: x_copy(c, ox).start())
        when(both(last_x, both(odd, y < ny - 1)), lambda: p_copy(c).start())
        when(both(both(last_x, dom == 0), c >= B_CH), lambda: t_copy(c - B_CH).start())

    def send_own():
        def own(c):
            z_copy(c, loc).start()

        each(A11_CH, B_CH, own)
        each(0, NA2, own)
        each(B_CH, NC, own)

    when(both(even, z == 0), send_own)

    @pl.when(both(even, z > 0))
    def _():
        def send(c):
            when(jnp.logical_not(gate), lambda: z_copy(c, oz).start())
            when(both(gate, x == 0), lambda: x_copy(c, oz).start())

        chain_a(ez, oz, wm, zr, send)
        when(both(gate, x > 0), lambda: put_weights(wt, oz))
        when(both(gate, x == 1), lambda: chain_a(ex, ox, wt, xr, x_send))
        chain_b(ez, oz, wm, loc, zr, send)

    @pl.when(both(odd, z == nz - 1))
    def _():
        def own_b(q):
            s_copy(B_CH + q, nloc).start()
            s_copy(B_CH + NB // 2 + q, nloc).start()

        each(0, B_CH, lambda c: s_copy(c, nloc).start())
        each(0, NB // 2, own_b)

    @pl.when(both(odd, jnp.logical_and(z > 0, z < nz - 1)))
    def _():
        def send(c):
            s_copy(c, os).start()

        back_top(es, os, send)
        back_low(es, os, send)
        back_b(es, os, send)

    @pl.when(both(odd, z == 0))
    def _():
        def send(c):
            when(c == 0, send_own)

        back_top(es, os, send)
        oz[A11_ROW:B_ROW, :] = stack(flip(os[0:H, 0 : 2 * H]))
        when(x == 0, lambda: each(A11_CH, B_CH, lambda c: x_copy(c, oz).start()))
        back_low(es, os, send)
        oz[0:H, 0 : 2 * H] = flip(os[0:H, 2 * H :])
        oz[0:H, 2 * H :] = flip(packed(os))
        when(x == 0, lambda: each(0, NA2, lambda c: x_copy(c, oz).start()))
        when(x > 0, lambda: put_weights(wt, oz))
        when(x == 1, lambda: chain_a(ex, ox, wt, xr, x_send))
        back_b(es, os, nothing)
        turn_b(os, oz)
        when(x == 0, lambda: each(B_CH, NC, lambda c: x_copy(c, oz).start()))

    @pl.when(both(gate, x > 0))
    def _():
        when(x > 1, lambda: chain_a(ex, ox, wt, xr, x_send))
        when(both(last_x, both(even, y > 0)), lambda: put_weights(wd, ox))
        chain_b(ex, ox, wt, oz, xr, x_send)
        put_weights(wex, ex)

    @pl.when(both(odd, z > 0))
    def _():
        @pl.when(z < nz - 1)
        def _():
            def send(c):
                z_copy(c, oz).start()

            chain_a(ez, oz, wm, zr, send)
            chain_b(ez, oz, wm, loc, zr, send)

        when(z == nz - 1, lambda: each(0, NC, lambda c: arrive(ez, zr, c)))

    when(z > 0, lambda: put_weights(we, ez))

    def spread(n, place, plus, buf, ssem, rsem, up, dn):
        def up_copy(c):
            return copy(buf, buf, c, ssem.at[0], rsem.at[c], up)

        def dn_copy(c):
            return copy(buf, buf, c, ssem.at[1], rsem.at[c], dn)

        to_up = jnp.logical_or(both(place == n - 1, plus > 0), place < plus - 1)
        to_dn = both(place > plus, plus < n - 1)

        def go(c):
            when(to_up, lambda: up_copy(c).start())
            when(to_dn, lambda: dn_copy(c).start())

        def drain():
            when(to_up, lambda: sent(buf, ssem.at[0]))
            when(to_dn, lambda: sent(buf, ssem.at[1]))

        return go, drain

    x_go, x_drain = spread(nx, x, (nx - 1) // 2, sd, xds, xdr, x_up, x_dn)
    z_place = jnp.where(odd, z + nz - 1, z) % nz
    z_go, z_drain = spread(nz, z_place, jnp.where(odd, nz // 2, (nz - 1) // 2), sx, zds, zdr, z_up, z_dn)

    def first_copy(c):
        return copy(op, ed, c, ds, dr.at[c], d_up, s_off=B_CH)

    def d_copy(c):
        return copy(od, ed, c, ds, dr.at[c], d_up)

    def f_copy(c):
        return copy(o1, sd, c, fs, xdr.at[c], twin)

    head = both(gate, last_x)
    even_head = both(head, even)

    @pl.when(even_head)
    def _():
        if ny > 1:
            @pl.when(y < ny - 1)
            def _():
                each(0, B_CH, lambda c: arrive(ep, pr, c))
                put_weights(wep, ep)

                @pl.when(y > 0)
                def _():
                    for r in (0, H // 2):
                        op[r : r + H // 2, :] = full(ox[r : r + H // 2, :], wep, mul3)
                    op[A11_ROW:B_ROW, :] = stack(mul3(packed(ox), wep, 0))
                    put_weights(wp, op)

                def pair(c):
                    b = rows(B_ROW + c * R, R)
                    arrive(ep, pr, c + B_CH)
                    op[b, :] = full(ox[b, :], wep, mul3) + ep[b, :]
                    when(y == 0, lambda: first_copy(c).start())

                each(0, NB, pair)

            def step(q):
                for half in range(2):
                    c = 2 * q + half
                    r, b = rows(c * R, R), rows(B_ROW + c * R, R)
                    arrive(ed, dr, c)

                    @pl.when(y < ny - 1)
                    def _():
                        od[r, :] = full(ed[r, :], wp, mul3) + op[b, :]
                        d_copy(c).start()

                    sd[r, :] = ed[r, :]
                    x_go(c)
                r, b = rows(2 * q * R, 2 * R), rows(B_ROW + 2 * q * R, 2 * R)
                o1[r, :] = full(ed[r, :], wd, mul3) + ox[b, :]
                for half in range(2):
                    f_copy(2 * q + half).start()

            when(y > 0, lambda: each(0, NB // 2, step))

        @pl.when(y == 0)
        def _():
            sd[...] = jnp.zeros_like(sd)
            each(0, NB, x_go)

    @pl.when(gate)
    def _():
        def step(c):
            r = rows(c * R, R)

            @pl.when(jnp.logical_not(even_head))
            def _():
                arrive(sd, xdr, c)
                x_go(c)

            @pl.when(x == 0)
            def _():
                sx[r, :] = sd[r, :]

            @pl.when(x > 0)
            def _():
                sx[r, :] = full(sd[r, :], wex, mul3) + ex[rows(B_ROW + c * R, R), :]

            z_go(c)

        each(0, NB, step)

    def finish(start, size):
        r = rows(start, size)

        @pl.when(z == 0)
        def _():
            fin[0, r, :] = sx[r, :]

        @pl.when(z > 0)
        def _():
            fin[0, r, :] = full(sx[r, :], we, mul3) + ez[rows(B_ROW + start, size), :]

        s0 = full(fin[0, r, :], wh.at[0], mul2) + inj[0, r, :]
        fin[0, r, :] = s0
        fin[1, r, :] = full(s0, wh.at[1], mul2) + inj[1, r, :]

    @pl.when(jnp.logical_not(gate))
    def _():
        def pass_on(c):
            arrive(sx, zdr, c)
            z_go(c)

        for half in range(2):
            each(half * (NB // 2), (half + 1) * (NB // 2), pass_on)
            finish(half * (H // 2), H // 2)

    when(gate, lambda: each(0, 2, lambda c: finish(c * (H // 2), H // 2)))

    for s in range(2):
        for p in range(2):
            for h in range(2):
                k = (2 * h + p) * H
                out[0, s, p, h * H : (h + 1) * H, :] = fin[s, :, k : k + H].T

    when(jnp.logical_or(z == 0, z < nz - 1), lambda: sent(ez, zs))
    when(both(odd, z > 0), lambda: sent(es, ss))
    when(both(gate, jnp.logical_or(jnp.logical_not(last_x), both(odd, y < ny - 1))), lambda: sent(ex, xs))
    when(even_head, lambda: sent(sd, fs))
    if ny > 1:
        when(both(even_head, y < ny - 1), lambda: sent(ed, ds))
    when(gate, x_drain)
    z_drain()


def build(mesh, nx):
    ndom, nrun = mesh.shape["dom"], mesh.shape["run"]
    nz = nrun // nx

    def shards(ainv, coupling, source):
        big = pltpu.VMEM((ROWS, 4 * H), F32)
        half = pltpu.VMEM((H, 4 * H), F32)
        weights = pltpu.VMEM((2, 6 * H, 2 * H), BF16)
        sem = pltpu.SemaphoreType.DMA

        def body(*refs):
            kernel(ndom, nx, nz, *refs)

        vm = pl.BlockSpec(memory_space=pltpu.VMEM)
        return pl.pallas_call(
            body,
            out_shape=jax.ShapeDtypeStruct(source.shape, F32),
            in_specs=[pl.BlockSpec(memory_space=pltpu.HBM)] * 3,
            out_specs=vm,
            scratch_shapes=[
                pltpu.VMEM((2, 2, 2 * H, 2 * H), BF16),
                pltpu.VMEM((2, 2, 2 * H, 2 * H), BF16),
                pltpu.VMEM((2, 2, 2 * H, H), BF16),
                sem((2, 3)),
                big, big, big, big, big, big, big, big, big, big,
                half, half, half, half, half,
                weights, weights, weights, weights, weights, weights, weights, weights,
                pltpu.VMEM((2, 4 * H, 2 * H), BF16),
                pltpu.VMEM((2, 6 * H, 2 * H), BF16),
                pltpu.VMEM((2, H, 4 * H), F32),
                pltpu.VMEM((2, H, 4 * H), F32),
                sem, sem((NC,)), sem, sem((NC,)), sem, sem((NC,)), sem((NC,)),
                sem, sem((NB,)), sem,
                sem((2,)), sem((NB,)), sem((2,)), sem((NB,)),
            ],
            compiler_params=pltpu.CompilerParams(
                collective_id=0, has_side_effects=True, vmem_limit_bytes=48 * 1024 * 1024
            ),
            name="sweep",
        )(*(pltpu.with_memory_space_constraint(a, pltpu.HBM) for a in (ainv, coupling, source)))

    in_specs = (
        P(None, ("dom", "run"), None, None, None),
        P(("dom", "run"), None, None, None),
        P(None, ("dom", "run"), None, None, None),
    )
    out_specs = P(None, ("dom", "run"), None, None, None)
    return jax.shard_map(shards, mesh=mesh, in_specs=in_specs, out_specs=out_specs, check_vma=False)


def solution(mesh):
    return build(mesh, NX)
```

```python
import jax
import jax.numpy as jnp
from jax import lax
from jax.experimental import pallas as pl
from jax.experimental.pallas import tpu as pltpu
from jax.sharding import PartitionSpec as P

MESH = pl.DeviceIdType.MESH
F32 = jnp.float32
BF16 = jnp.bfloat16

NX = 4
H = 128
R = 16
NA2 = H // R
NA11 = H // 2 // R
NB = H // R
A11_ROW = H
B_ROW = H + H // 2
ROWS = B_ROW + H
A11_CH = NA2
B_CH = NA2 + NA11
NC = B_CH + NB


def dot(a, b):
    return lax.dot_general(a, b, (((1,), (0,)), ((), ())), preferred_element_type=F32)


def split(x):
    hi = x.astype(BF16)
    return hi, (x - hi.astype(F32)).astype(BF16)


def rows(start, size):
    return pl.ds(pl.multiple_of(start, 8), size)


def put_tile(w, t, top):
    k = t * 2 * H
    w[k : k + H, :] = top
    w[k + H : k + 2 * H, 0:H] = -top[:, H:]
    w[k + H : k + 2 * H, H:] = top[:, :H]


def tile(t, n=1):
    return slice(t * 2 * H, (t + n) * 2 * H)


def put_pair(w, t, top):
    hi, lo = split(top)
    put_tile(w.at[0], t, hi)
    put_tile(w.at[1], t, lo)


def unstack(v):
    return jnp.concatenate([v[:, : 2 * H], v[:, 2 * H :]], axis=0)


def stack(y):
    n = y.shape[0] // 2
    return jnp.concatenate([y[:n], y[n:]], axis=1)


def packed(buf):
    return unstack(buf[A11_ROW:B_ROW, :])


def put_weights(w, buf):
    put_pair(w, 0, packed(buf))
    put_pair(w, 1, buf[0:H, 0 : 2 * H])
    put_pair(w, 2, buf[0:H, 2 * H :])


def put_weights_n(w, wb, buf):
    put_pair(w, 0, buf[0:H, 0 : 2 * H])
    put_pair(w, 1, buf[0:H, 2 * H :])
    put_pair(w, 2, packed(buf))
    put_pair(wb, 0, buf[B_ROW:, 0 : 2 * H])
    put_pair(wb, 1, buf[B_ROW:, 2 * H :])


def flip(v):
    return jnp.concatenate([v[:, k : k + H].T for k in range(0, v.shape[1], H)], axis=1)


def turn_a(src, dst):
    dst[0:H, 0 : 2 * H] = flip(packed(src))
    dst[0:H, 2 * H :] = flip(src[0:H, 0 : 2 * H])
    dst[A11_ROW:B_ROW, :] = stack(flip(src[0:H, 2 * H :]))


def turn_b(src, dst):
    dst[B_ROW:, :] = flip(src[B_ROW:, :])


def mul3(x, w, t, k=1):
    n = x.shape[0]
    hi, lo = split(x)
    both = dot(jnp.concatenate([hi, lo], axis=0), w[0, tile(t, k), :])
    return both[:n] + both[n:] + dot(hi, w[1, tile(t, k), :])


def mul2(x, w, t, k=1):
    n = x.shape[0]
    hi, lo = split(x)
    both = dot(jnp.concatenate([hi, lo], axis=0), w[tile(t, k), :])
    return both[:n] + both[n:]


def full(x, w, mul):
    return jnp.concatenate([mul(x, w, 0, 2), mul(x[:, 2 * H :], w, 2)], axis=1)


def kernel(
    ndom, nx, nz, ainv_in, coup_in, src_in, out,
    ainv, coup, src, in_sem,
    loc, ez, oz, ex, ox, es, os, nloc, ep, op, ed, od, o1, sd, sx,
    wm, we, wt, wex, wd, wn, wp, wep, wb, wh, inj, fin,
    zs, zr, xs, xr, ss, sr, pr, ds, dr, fs, xds, xdr, zds, zdr,
):
    loads = []
    for s in range(2):
        loads.append([
            pltpu.make_async_copy(ainv_in.at[0, s], ainv.at[s], in_sem.at[s, 0]),
            pltpu.make_async_copy(coup_in.at[s], coup.at[s], in_sem.at[s, 1]),
            pltpu.make_async_copy(src_in.at[0, s], src.at[s], in_sem.at[s, 2]),
        ])
        for load in loads[s]:
            load.start()
    dom, run = lax.axis_index("dom"), lax.axis_index("run")
    x, z = run // nz, run % nz
    y, odd = dom // 2, dom % 2 == 1
    even = jnp.logical_not(odd)
    ny = ndom // 2
    gate = jnp.where(odd, z == 0, z == nz - 1)
    last_x = x == nx - 1
    both = jnp.logical_and

    def at(d, xx, zz):
        return (d, xx * nz + zz)

    z_up, z_dn = at(dom, x, (z + 1) % nz), at(dom, x, (z + nz - 1) % nz)
    x_up, x_dn = at(dom, (x + 1) % nx, z), at(dom, (x + nx - 1) % nx, z)
    d_up, d_dn = at((dom + 2) % ndom, x, z), at((dom + ndom - 2) % ndom, x, z)
    twin = at(dom + 1 - 2 * (dom % 2), x, jnp.where(odd, z + nz - 1, z + 1) % nz)

    barrier = pltpu.get_barrier_semaphore()
    greet = (z_up, z_dn, x_up, x_dn, twin) + ((d_up, d_dn) if ny > 1 else ())
    for who in greet:
        pl.semaphore_signal(barrier, inc=1, device_id=who, device_id_type=MESH)

    for s in range(2):
        for load in loads[s]:
            load.wait()
        ar, ai = ainv[s, 0], ainv[s, 1]
        cr, ci = coup[s, 0], coup[s, 1]
        hr = (dot(ai, ci) - dot(ar, cr)).astype(BF16).astype(F32)
        hi = (-(dot(ar, ci) + dot(ai, cr))).astype(BF16).astype(F32)
        for t, (i, j) in enumerate(((0, 0), (0, H), (H, H))):
            top = jnp.concatenate(
                [hr[i : i + H, j : j + H].T, hi[i : i + H, j : j + H].T], axis=1
            )
            put_tile(wh.at[s], t, top.astype(BF16))
        sr_, si_ = src[s, 0], src[s, 1]
        pr_ = dot(ar, sr_) - dot(ai, si_)
        pi_ = dot(ar, si_) + dot(ai, sr_)
        for h in range(2):
            inj[s, :, 2 * h * H : (2 * h + 1) * H] = pr_[h * H : (h + 1) * H].T
            inj[s, :, (2 * h + 1) * H : (2 * h + 2) * H] = pi_[h * H : (h + 1) * H].T
    w1 = wh.at[1]
    tops = [wh[0, t * 2 * H : t * 2 * H + H, :] for t in range(3)]
    loc[A11_ROW:B_ROW, :] = stack(dot(tops[0], w1[tile(0), :]))
    loc[0:H, : 2 * H] = dot(jnp.concatenate([tops[1], tops[2]], axis=1), w1[tile(0, 2), :])
    loc[0:H, 2 * H :] = dot(tops[2], w1[tile(2), :])
    loc[B_ROW:, :] = full(inj[0], w1, mul2) + inj[1]

    @pl.when(odd)
    def _():
        turn_a(loc, nloc)
        turn_b(loc, nloc)

    pl.semaphore_wait(barrier, len(greet))

    def copy(src_ref, dst_ref, c, ssem, rsem, who, s_off=0):
        return pltpu.make_async_remote_copy(
            src_ref=src_ref.at[rows((c + s_off) * R, R)], dst_ref=dst_ref.at[rows(c * R, R)],
            send_sem=ssem, recv_sem=rsem, device_id=who, device_id_type=MESH,
        )

    def sent(buf, ssem):
        pltpu.make_async_remote_copy(
            src_ref=buf, dst_ref=buf, send_sem=ssem, recv_sem=zr.at[0],
            device_id=z_up, device_id_type=MESH,
        ).wait_send()

    def arrive(buf, rsem, c):
        copy(buf, buf, c, zs, rsem.at[c], z_up).wait_recv()

    def each(lo, hi, body):
        def step(c, carry):
            body(c)
            return carry

        lax.fori_loop(lo, hi, step, 0)

    def when(cond, body):
        pl.when(cond)(body)

    def chain_a(inp, outp, w, rsem, send):
        def a2(c):
            arrive(inp, rsem, c)
            outp[rows(c * R, R), :] = full(inp[rows(c * R, R), :], w, mul3)
            send(c)

        def a11(c):
            arrive(inp, rsem, c)
            outp[rows(c * R, R), :] = stack(mul3(unstack(inp[rows(c * R, R), :]), w, 0))
            send(c)

        each(A11_CH, B_CH, a11)
        each(0, NA2, a2)

    def chain_b(inp, outp, w, own, rsem, send):
        def bb(c):
            arrive(inp, rsem, c)
            r = rows(c * R, R)
            outp[r, :] = full(inp[r, :], w, mul3) + own[r, :]
            send(c)

        each(B_CH, NC, bb)

    def back_top(inp, outp, send):
        def top(c):
            arrive(inp, sr, c)
            v = inp[rows(c * R, R), :]
            outp[rows(c * R, R), :] = jnp.concatenate(
                [mul3(v[:, : 2 * H], wn, 0), mul3(v, wn, 1, 2)], axis=1
            )
            send(c)

        each(0, NA2, top)

    def back_low(inp, outp, send):
        def low(c):
            arrive(inp, sr, c)
            outp[rows(c * R, R), :] = stack(mul3(unstack(inp[rows(c * R, R), :]), wn, 2))
            send(c)

        each(A11_CH, B_CH, low)

    def back_b(inp, outp, send):
        def bb(q):
            for half in range(2):
                k = q + half * (NB // 2)
                c = B_CH + k
                arrive(inp, sr, c)
                v = inp[rows(k * R, R), :]
                low = inp[rows(A11_ROW + q * R, R), half * 2 * H : (half + 1) * 2 * H]
                y1 = mul3(v, wb, 0, 2)
                y2 = mul3(low, wb, 1)
                r = rows(c * R, R)
                outp[r, :] = jnp.concatenate([y1, y2], axis=1) + inp[r, :]
                send(c)

        each(0, NB // 2, bb)

    def z_copy(c, src_ref):
        return copy(src_ref, ez, c, zs, zr.at[c], z_up)

    def s_copy(c, src_ref):
        return copy(src_ref, es, c, ss, sr.at[c], z_dn)

    def x_copy(c, src_ref):
        return copy(src_ref, ex, c, xs, xr.at[c], x_up)

    def p_copy(c):
        return copy(ox, ep, c, xs, pr.at[c], twin)

    def nothing(c):
        pass

    def t_copy(c):
        return copy(ox, sd, c, fs, xdr.at[c], twin, s_off=B_CH)

    def x_send(c):
        when(jnp.logical_not(last_x), lambda: x_copy(c, ox).start())
        when(both(last_x, both(odd, y < ny - 1)), lambda: p_copy(c).start())
        when(both(both(last_x, dom == 0), c >= B_CH), lambda: t_copy(c - B_CH).start())

    def send_own():
        def own(c):
            z_copy(c, loc).start()

        each(A11_CH, B_CH, own)
        each(0, NA2, own)
        each(B_CH, NC, own)

    when(both(even, z == 0), send_own)

    @pl.when(both(odd, z == nz - 1))
    def _():
        def own_b(q):
            s_copy(B_CH + q, nloc).start()
            s_copy(B_CH + NB // 2 + q, nloc).start()

        each(0, B_CH, lambda c: s_copy(c, nloc).start())
        each(0, NB // 2, own_b)

    put_weights(wm, loc)
    when(odd, lambda: put_weights_n(wn, wb, nloc))

    @pl.when(both(even, z > 0))
    def _():
        def send(c):
            when(jnp.logical_not(gate), lambda: z_copy(c, oz).start())
            when(both(gate, x == 0), lambda: x_copy(c, oz).start())

        chain_a(ez, oz, wm, zr, send)
        when(both(gate, x > 0), lambda: put_weights(wt, oz))
        when(both(gate, x == 1), lambda: chain_a(ex, ox, wt, xr, x_send))
        chain_b(ez, oz, wm, loc, zr, send)

    @pl.when(both(odd, jnp.logical_and(z > 0, z < nz - 1)))
    def _():
        def send(c):
            s_copy(c, os).start()

        back_top(es, os, send)
        back_low(es, os, send)
        back_b(es, os, send)

    @pl.when(both(odd, z == 0))
    def _():
        def send(c):
            when(c == 0, send_own)

        back_top(es, os, send)
        oz[A11_ROW:B_ROW, :] = stack(flip(os[0:H, 0 : 2 * H]))
        when(x == 0, lambda: each(A11_CH, B_CH, lambda c: x_copy(c, oz).start()))
        back_low(es, os, send)
        oz[0:H, 0 : 2 * H] = flip(os[0:H, 2 * H :])
        oz[0:H, 2 * H :] = flip(packed(os))
        when(x == 0, lambda: each(0, NA2, lambda c: x_copy(c, oz).start()))
        when(x > 0, lambda: put_weights(wt, oz))
        when(x == 1, lambda: chain_a(ex, ox, wt, xr, x_send))
        back_b(es, os, nothing)
        turn_b(os, oz)
        when(x == 0, lambda: each(B_CH, NC, lambda c: x_copy(c, oz).start()))

    @pl.when(both(gate, x > 0))
    def _():
        when(x > 1, lambda: chain_a(ex, ox, wt, xr, x_send))
        when(both(last_x, both(even, y > 0)), lambda: put_weights(wd, ox))
        chain_b(ex, ox, wt, oz, xr, x_send)
        put_weights(wex, ex)

    @pl.when(both(odd, z > 0))
    def _():
        @pl.when(z < nz - 1)
        def _():
            def send(c):
                z_copy(c, oz).start()

            chain_a(ez, oz, wm, zr, send)
            chain_b(ez, oz, wm, loc, zr, send)

        when(z == nz - 1, lambda: each(0, NC, lambda c: arrive(ez, zr, c)))

    when(z > 0, lambda: put_weights(we, ez))

    def spread(n, place, plus, buf, ssem, rsem, up, dn):
        def up_copy(c):
            return copy(buf, buf, c, ssem.at[0], rsem.at[c], up)

        def dn_copy(c):
            return copy(buf, buf, c, ssem.at[1], rsem.at[c], dn)

        to_up = jnp.logical_or(both(place == n - 1, plus > 0), place < plus - 1)
        to_dn = both(place > plus, plus < n - 1)

        def go(c):
            when(to_up, lambda: up_copy(c).start())
            when(to_dn, lambda: dn_copy(c).start())

        def drain():
            when(to_up, lambda: sent(buf, ssem.at[0]))
            when(to_dn, lambda: sent(buf, ssem.at[1]))

        return go, drain

    x_go, x_drain = spread(nx, x, (nx - 1) // 2, sd, xds, xdr, x_up, x_dn)
    z_place = jnp.where(odd, z + nz - 1, z) % nz
    z_go, z_drain = spread(nz, z_place, jnp.where(odd, nz // 2, (nz - 1) // 2), sx, zds, zdr, z_up, z_dn)

    def first_copy(c):
        return copy(op, ed, c, ds, dr.at[c], d_up, s_off=B_CH)

    def d_copy(c):
        return copy(od, ed, c, ds, dr.at[c], d_up)

    def f_copy(c):
        return copy(o1, sd, c, fs, xdr.at[c], twin)

    head = both(gate, last_x)
    even_head = both(head, even)

    @pl.when(even_head)
    def _():
        if ny > 1:
            @pl.when(y < ny - 1)
            def _():
                each(0, B_CH, lambda c: arrive(ep, pr, c))
                put_weights(wep, ep)

                @pl.when(y > 0)
                def _():
                    for r in (0, H // 2):
                        op[r : r + H // 2, :] = full(ox[r : r + H // 2, :], wep, mul3)
                    op[A11_ROW:B_ROW, :] = stack(mul3(packed(ox), wep, 0))
                    put_weights(wp, op)

                def pair(c):
                    b = rows(B_ROW + c * R, R)
                    arrive(ep, pr, c + B_CH)
                    op[b, :] = full(ox[b, :], wep, mul3) + ep[b, :]
                    when(y == 0, lambda: first_copy(c).start())

                each(0, NB, pair)

            def step(q):
                for half in range(2):
                    c = 2 * q + half
                    r, b = rows(c * R, R), rows(B_ROW + c * R, R)
                    arrive(ed, dr, c)

                    @pl.when(y < ny - 1)
                    def _():
                        od[r, :] = full(ed[r, :], wp, mul3) + op[b, :]
                        d_copy(c).start()

                    sd[r, :] = ed[r, :]
                    x_go(c)

                    @pl.when(y == ny - 1)
                    def _():
                        o1[r, :] = full(ed[r, :], wd, mul3) + ox[b, :]
                        f_copy(c).start()

                @pl.when(y < ny - 1)
                def _():
                    r, b = rows(2 * q * R, 2 * R), rows(B_ROW + 2 * q * R, 2 * R)
                    o1[r, :] = full(ed[r, :], wd, mul3) + ox[b, :]
                    for half in range(2):
                        f_copy(2 * q + half).start()

            when(y > 0, lambda: each(0, NB // 2, step))

        @pl.when(y == 0)
        def _():
            sd[...] = jnp.zeros_like(sd)
            each(0, NB, x_go)

    @pl.when(gate)
    def _():
        def step(c):
            r = rows(c * R, R)

            @pl.when(jnp.logical_not(even_head))
            def _():
                arrive(sd, xdr, c)
                x_go(c)

            @pl.when(x == 0)
            def _():
                sx[r, :] = sd[r, :]

            @pl.when(x > 0)
            def _():
                sx[r, :] = full(sd[r, :], wex, mul3) + ex[rows(B_ROW + c * R, R), :]

            z_go(c)

        each(0, NB, step)

    def finish(start, size):
        r = rows(start, size)

        @pl.when(z == 0)
        def _():
            fin[0, r, :] = sx[r, :]

        @pl.when(z > 0)
        def _():
            fin[0, r, :] = full(sx[r, :], we, mul3) + ez[rows(B_ROW + start, size), :]

        s0 = full(fin[0, r, :], wh.at[0], mul2) + inj[0, r, :]
        fin[0, r, :] = s0
        fin[1, r, :] = full(s0, wh.at[1], mul2) + inj[1, r, :]

    when(jnp.logical_or(z == 0, z < nz - 1), lambda: sent(ez, zs))
    when(both(odd, z > 0), lambda: sent(es, ss))

    @pl.when(jnp.logical_not(gate))
    def _():
        def pass_on(c):
            arrive(sx, zdr, c)
            z_go(c)

        for half in range(2):
            each(half * (NB // 2), (half + 1) * (NB // 2), pass_on)
            finish(half * (H // 2), H // 2)

    when(gate, lambda: each(0, 2, lambda c: finish(c * (H // 2), H // 2)))

    for s in range(2):
        for p in range(2):
            for h in range(2):
                k = (2 * h + p) * H
                out[0, s, p, h * H : (h + 1) * H, :] = fin[s, :, k : k + H].T

    when(both(gate, jnp.logical_or(jnp.logical_not(last_x), both(odd, y < ny - 1))), lambda: sent(ex, xs))
    when(even_head, lambda: sent(sd, fs))
    if ny > 1:
        when(both(even_head, y < ny - 1), lambda: sent(ed, ds))
    when(gate, x_drain)
    z_drain()


def build(mesh, nx):
    ndom, nrun = mesh.shape["dom"], mesh.shape["run"]
    nz = nrun // nx

    def shards(ainv, coupling, source):
        big = pltpu.VMEM((ROWS, 4 * H), F32)
        half = pltpu.VMEM((H, 4 * H), F32)
        weights = pltpu.VMEM((2, 6 * H, 2 * H), BF16)
        sem = pltpu.SemaphoreType.DMA

        def body(*refs):
            kernel(ndom, nx, nz, *refs)

        vm = pl.BlockSpec(memory_space=pltpu.VMEM)
        return pl.pallas_call(
            body,
            out_shape=jax.ShapeDtypeStruct(source.shape, F32),
            in_specs=[pl.BlockSpec(memory_space=pltpu.HBM)] * 3,
            out_specs=vm,
            scratch_shapes=[
                pltpu.VMEM((2, 2, 2 * H, 2 * H), BF16),
                pltpu.VMEM((2, 2, 2 * H, 2 * H), BF16),
                pltpu.VMEM((2, 2, 2 * H, H), BF16),
                sem((2, 3)),
                big, big, big, big, big, big, big, big, big, big,
                half, half, half, half, half,
                weights, weights, weights, weights, weights, weights, weights, weights,
                pltpu.VMEM((2, 4 * H, 2 * H), BF16),
                pltpu.VMEM((2, 6 * H, 2 * H), BF16),
                pltpu.VMEM((2, H, 4 * H), F32),
                pltpu.VMEM((2, H, 4 * H), F32),
                sem, sem((NC,)), sem, sem((NC,)), sem, sem((NC,)), sem((NC,)),
                sem, sem((NB,)), sem,
                sem((2,)), sem((NB,)), sem((2,)), sem((NB,)),
            ],
            compiler_params=pltpu.CompilerParams(
                collective_id=0, has_side_effects=True, vmem_limit_bytes=48 * 1024 * 1024
            ),
            name="sweep",
        )(*(pltpu.with_memory_space_constraint(a, pltpu.HBM) for a in (ainv, coupling, source)))

    in_specs = (
        P(None, ("dom", "run"), None, None, None),
        P(("dom", "run"), None, None, None),
        P(None, ("dom", "run"), None, None, None),
    )
    out_specs = P(None, ("dom", "run"), None, None, None)
    return jax.shard_map(shards, mesh=mesh, in_specs=in_specs, out_specs=out_specs, check_vma=False)


def solution(mesh):
    return build(mesh, NX)
```
